128 devices in a mesh: req: 8 (over y, core), exp: 16 (over z, x).
Axes of the slice: x: 4, y: 4, z: 4, core: 2. Of those that a mesh axis runs over, the one named last changes fastest.
Arguments:
- resid: bfloat16 [8192, 2048], P(('req', 'exp')), may hold values from -27 to 27
- queries: bfloat16 [8192, 2048], P(('req', 'exp')), may hold values from -6 to 6
- cache_key: bfloat16 [256, 128, 2048], P(('req', 'exp')), may hold values from -6 to 6
- cache_value: bfloat16 [256, 128, 2048], P(('req', 'exp')), may hold values from -6 to 6
- page_table: int32 [32, 8], P('req'), may hold values from 0 to 31, as said below
- row_request: int32 [8192], P('req'), may hold values from 0 to 3, as said below
- row_position: int32 [8192], P('req'), may hold values from 0 to 1023, as said below
- out_proj: bfloat16 [2048, 2048], P('exp'), may hold values from -0.375 to 0.375
- norm_gain: float32 [2048], replicated, may hold values from 0.5 to 1.5
- expert_gate: bfloat16 [128, 2048, 1408], P(('req', 'exp')), as said below
- expert_up: bfloat16 [128, 2048, 1408], P(('req', 'exp')), as said below
- expert_down: bfloat16 [128, 1408, 2048], P(('req', 'exp')), as said below
- shared_gate: bfloat16 [2048, 5632], P(None, 'exp'), may hold values from -0.125 to 0.125
- shared_up: bfloat16 [2048, 5632], P(None, 'exp'), may hold values from -0.125 to 0.125
- shared_down: bfloat16 [5632, 2048], P('exp'), may hold values from -0.078125 to 0.078125
- shared_scalar: bfloat16 [2048], replicated, may hold values from -0.375 to 0.375
- slot_expert: int32 [128], replicated, may hold values from 0 to 59, as said below
- route_expert: int32 [8192, 4], replicated, may hold values from 0 to 59, as said below
- route_gate: float32 [8192, 4], P(('req', 'exp')), may hold values from 0.05 to 0.5
Outputs:
- output: bfloat16 [8192, 2048], P(('req', 'exp'))
The draws below stay inside these ranges and needn't reach their ends.
Inputs may be any that keep to these rules, and one draw needn't show every extreme that they name: `page_table`: within each request group the table names each of the group's 32 pages once; page p of group g lies on the device of req index g and exp index p // 2. `row_request`: each group's rows are in order of request; every request has one row or more; half of the requests of a group have exactly one row. `row_position`: the rows of one request hold consecutive positions ending at the request's length minus one. `slot_expert`: every expert is held by one slot or more. `route_expert`: each row names 4 different experts. In each aligned block of 64 rows (the rows of one device) no expert is named more than 6 times, and one expert is named exactly 6 times in every block. `expert_gate`: slots that hold the same expert hold equal weights. `expert_up`: slots that hold the same expert hold equal weights. `expert_down`: slots that hold the same expert hold equal weights.
All inputs are finite; a program needn't handle non-finite values.
Results may differ from the reference program's by a relative error of at most 0.006.
Values may be sent and summed in bfloat16 or wider, within the bound.
A program may use at most 128 MiB of HBM per device.

```python
import math
import jax
import jax.numpy as jnp
from jax import lax

D = 2048
HEADS = 16
HEAD_DIM = 128
FF = 1408
SH_FF = 5632
TOPK = 4
PAGE = 128
TOK_DEV = 64
REQS_G = 4
GROUPS = 8
GROUP_ROWS = 1024
ROWS = 8192
SLOTS = 128
EXPERTS = 60
CAP = 6
PAGES_G = 32
MAXP = 8


def group_layout(key):
    half = REQS_G // 2
    key_order, key_spread, key_length, key_table = jax.random.split(key, 4)
    requests = jax.random.permutation(key_order, REQS_G).astype(jnp.int32)
    prefill_total = GROUP_ROWS - half
    base = prefill_total // half
    spread = jax.random.randint(key_spread, (half // 2,), -(base // 4), base // 4 + 1)
    deltas = jnp.stack([spread, -spread], axis=1).reshape(-1)
    prefill_counts = (base + deltas).at[half - 1].add(prefill_total - base * half).astype(jnp.int32)
    counts = jnp.zeros((REQS_G,), jnp.int32).at[requests[:half]].set(1).at[requests[half:]].set(prefill_counts)
    full = MAXP * PAGE
    lengths = jax.random.randint(key_length, (REQS_G,), counts, full + 1).astype(jnp.int32)
    lengths = lengths.at[requests[0]].set(full).at[requests[half]].set(counts[requests[half]])
    starts = jnp.cumsum(counts) - counts
    row_ids = jnp.arange(GROUP_ROWS, dtype=jnp.int32)
    request = jnp.sum((row_ids[:, None] >= starts[None, :]).astype(jnp.int32), axis=1) - 1
    position = lengths[request] - counts[request] + row_ids - starts[request]
    table = jax.random.permutation(key_table, PAGES_G).astype(jnp.int32).reshape(REQS_G, MAXP)
    return (table, request.astype(jnp.int32), position.astype(jnp.int32))


def all_layouts(key):
    base_key = jax.random.fold_in(key, 11)
    return jax.vmap(lambda group: group_layout(jax.random.fold_in(base_key, group)))(jnp.arange(GROUPS))


def draw_page_table(key, part):
    return all_layouts(key)[0].reshape(GROUPS * REQS_G, MAXP)


def draw_row_request(key, part):
    return all_layouts(key)[1].reshape(ROWS)


def draw_row_position(key, part):
    return all_layouts(key)[2].reshape(ROWS)


def hot_expert(key):
    return jax.random.randint(jax.random.fold_in(key, 3), (), 0, EXPERTS)


def draw_slot_expert(key, part):
    key_pick, key_order = jax.random.split(jax.random.fold_in(key, 5))
    extra = SLOTS - EXPERTS
    picks = jax.random.randint(key_pick, (extra,), 0, EXPERTS)
    picks = jnp.where(jnp.arange(extra) % 4 == 0, hot_expert(key), picks)
    holders = jnp.concatenate([jnp.arange(EXPERTS), picks]).astype(jnp.int32)
    return jax.random.permutation(key_order, holders)


def draw_route_expert(key, part):
    hot = hot_expert(key)
    others = (hot + 1 + jnp.arange(EXPERTS - 1)) % EXPERTS
    block_key = jax.random.fold_in(key, 17)

    def block(index):
        key_map, key_rows = jax.random.split(jax.random.fold_in(block_key, index))
        mapping = jax.random.permutation(key_map, others)
        cycle = (jnp.arange(TOK_DEV)[:, None] * TOPK + jnp.arange(TOPK)[None, :]) % (EXPERTS - 1)
        chosen = mapping[cycle]
        marked = jnp.zeros((TOK_DEV,), jnp.int32).at[jax.random.permutation(key_rows, TOK_DEV)[:CAP]].set(1)
        first = jnp.where(marked == 1, hot, chosen[:, 0])
        return jnp.concatenate([first[:, None], chosen[:, 1:]], axis=1).astype(jnp.int32)
    return jax.vmap(block)(jnp.arange(SLOTS)).reshape(ROWS, TOPK)


def expert_tensor(key, salt, shape, fan_in):
    holders = draw_slot_expert(key, 0)
    salt_key = jax.random.fold_in(key, salt)

    def one(expert):
        values = jax.random.normal(jax.random.fold_in(salt_key, expert), shape, jnp.float32)
        return jnp.clip(values, -6.0, 6.0) * fan_in ** (-0.5)
    return jax.vmap(one)(holders)


def draw_expert_gate(key, part):
    return expert_tensor(key, 41, (D, FF), D).astype(jnp.bfloat16)


def draw_expert_up(key, part):
    return expert_tensor(key, 43, (D, FF), D).astype(jnp.bfloat16)


def draw_expert_down(key, part):
    return expert_tensor(key, 47, (FF, D), FF).astype(jnp.bfloat16)


def draw_queries(key, part):
    noise_key = jax.random.fold_in(key, 21)
    return jnp.clip(1.5 * jax.random.normal(noise_key, (ROWS, D), jnp.float32), -6.0, 6.0).astype(jnp.bfloat16)


def draw_cache_key(key, part):
    noise_key = jax.random.fold_in(key, 23)
    shape = (GROUPS * PAGES_G, PAGE, D)
    return jnp.clip(jax.random.normal(noise_key, shape, jnp.float32), -6.0, 6.0).astype(jnp.bfloat16)


def draw_resid(key, part):
    key_rows, key_cols, key_noise = jax.random.split(jax.random.fold_in(key, 31), 3)
    low = math.log(0.3)
    high = math.log(3.0)
    row_scale = jnp.exp(jax.random.uniform(key_rows, (ROWS, 1), jnp.float32, low, high))
    col_scale = jnp.exp(jax.random.uniform(key_cols, (1, D), jnp.float32, low, high))
    noise = jnp.clip(jax.random.normal(key_noise, (ROWS, D), jnp.float32), -3.0, 3.0)
    return (noise * row_scale * col_scale).astype(jnp.bfloat16)


def shard_levels(stream_key, dims, cuts, least, high):
    def one(axis_at, blocks):
        steps = jax.random.uniform(jax.random.fold_in(jax.random.fold_in(stream_key, 6), axis_at), (blocks,), jnp.float32, least / len(cuts), high / len(cuts))
        return jnp.repeat(jnp.exp(steps), dims[axis_at] // blocks).reshape((-1,) + (1,) * (len(dims) - axis_at - 1))

    factor_of = one(*cuts[0])
    for cut in cuts[1:]:
        factor_of = factor_of * one(*cut)
    return factor_of


def scatter_about(own_key, extent, scale, most, pieces=(), kind=jnp.bfloat16):
    drawn = scale * jax.random.normal(own_key, extent, jnp.float32)
    if pieces:
        drawn = drawn * shard_levels(own_key, extent, pieces, -0.22, 0.18)
    return jnp.clip(drawn, -most, most).astype(kind)


def setup_inputs(seed: int = 0) -> dict:
    splits = jax.random.split(jax.random.key(seed), 20)
    resid = draw_resid(jax.random.fold_in(splits[19], 71), 0)
    queries = draw_queries(jax.random.fold_in(splits[19], 71), 0)
    cache_key = draw_cache_key(jax.random.fold_in(splits[19], 71), 0)
    cache_value = scatter_about(splits[3], (GROUPS * PAGES_G, PAGE, D), 1.0, 6.0, ((0, 128),))
    page_table = draw_page_table(jax.random.fold_in(splits[19], 71), 0)
    row_request = draw_row_request(jax.random.fold_in(splits[19], 71), 0)
    row_position = draw_row_position(jax.random.fold_in(splits[19], 71), 0)
    out_proj = scatter_about(splits[7], (D, D), (D // 8) ** -0.5, 0.375, ((0, 16),))
    norm_gain = jnp.clip(1.0 + 0.1 * jax.random.normal(splits[8], (D,), jnp.float32), 0.5, 1.5)
    expert_gate = draw_expert_gate(jax.random.fold_in(splits[19], 71), 0)
    expert_up = draw_expert_up(jax.random.fold_in(splits[19], 71), 0)
    expert_down = draw_expert_down(jax.random.fold_in(splits[19], 71), 0)
    shared_gate = scatter_about(splits[12], (D, SH_FF), D ** -0.5, 0.125, ((1, 16),))
    shared_up = scatter_about(splits[13], (D, SH_FF), D ** -0.5, 0.125, ((1, 16),))
    shared_down = scatter_about(splits[14], (SH_FF, D), SH_FF ** -0.5, 0.078125, ((0, 16),))
    shared_scalar = scatter_about(splits[15], (D,), (D // 8) ** -0.5, 0.375)
    slot_expert = draw_slot_expert(jax.random.fold_in(splits[19], 71), 0)
    route_expert = draw_route_expert(jax.random.fold_in(splits[19], 71), 0)
    route_gate = jnp.clip(jnp.exp(math.log(0.5) - 2.3025851 * jax.random.uniform(splits[18], (ROWS, TOPK), jnp.float32) ** shard_levels(splits[18], (ROWS, TOPK), ((0, 128),), -0.2, 0.2)), 0.05, 0.5)
    return dict(resid=resid, queries=queries, cache_key=cache_key, cache_value=cache_value, page_table=page_table, row_request=row_request, row_position=row_position, out_proj=out_proj, norm_gain=norm_gain, expert_gate=expert_gate, expert_up=expert_up, expert_down=expert_down, shared_gate=shared_gate, shared_up=shared_up, shared_down=shared_down, shared_scalar=shared_scalar, slot_expert=slot_expert, route_expert=route_expert, route_gate=route_gate)


def expert_block(rows, gate_w, up_w, down_w):
    gate = jnp.dot(rows, gate_w, preferred_element_type=jnp.float32)
    upper = jnp.dot(rows, up_w, preferred_element_type=jnp.float32)
    hidden = (jax.nn.silu(gate) * upper).astype(jnp.bfloat16)
    return jnp.dot(hidden, down_w, preferred_element_type=jnp.float32).astype(jnp.bfloat16)

def group_attention(inputs):
    query_rows, keys, values, table, request, position = inputs
    page_ids = jnp.arange(PAGES_G, dtype=jnp.int32)
    hits = (table[None, :, :] == page_ids[:, None, None]).astype(jnp.int32)
    page_request = lax.optimization_barrier(jnp.sum(hits * jnp.arange(REQS_G, dtype=jnp.int32)[None, :, None], axis=(1, 2)))
    page_slot = lax.optimization_barrier(jnp.sum(hits * jnp.arange(MAXP, dtype=jnp.int32)[None, None, :], axis=(1, 2)))
    key_position = (page_slot[:, None] * PAGE + jnp.arange(PAGE, dtype=jnp.int32)[None, :]).reshape(-1)
    key_request = jnp.repeat(page_request, PAGE)
    visible = (request[:, None] == key_request[None, :]) & (key_position[None, :] <= position[:, None])
    query_heads = query_rows.astype(jnp.float32).reshape(GROUP_ROWS, HEADS, HEAD_DIM)
    key_heads = keys.astype(jnp.float32).reshape(PAGES_G * PAGE, HEADS, HEAD_DIM)
    value_heads = values.astype(jnp.float32).reshape(PAGES_G * PAGE, HEADS, HEAD_DIM)
    scores = jnp.einsum('rhd,khd->hrk', query_heads, key_heads) * HEAD_DIM ** (-0.5)
    scores = jnp.where(visible[None], scores, -1e+30)
    top = lax.optimization_barrier(jnp.max(scores, axis=2))
    weights = jnp.where(visible[None], jnp.exp(scores - top[:, :, None]), 0.0)
    denominators = jnp.transpose(lax.optimization_barrier(jnp.sum(weights, axis=2)))
    rounded = weights.astype(jnp.bfloat16).astype(jnp.float32)
    numerators = jnp.einsum('hrk,khd->rhd', rounded, value_heads)
    attention = numerators / denominators[:, :, None]
    return attention.reshape(GROUP_ROWS, D).astype(jnp.bfloat16)

def reference(resid, queries, cache_key, cache_value, page_table, row_request, row_position, out_proj, norm_gain, expert_gate, expert_up, expert_down, shared_gate, shared_up, shared_down, shared_scalar, slot_expert, route_expert, route_gate):
    attention = lax.map(group_attention, (queries.reshape(GROUPS, GROUP_ROWS, D), cache_key.reshape(GROUPS, PAGES_G, PAGE, D), cache_value.reshape(GROUPS, PAGES_G, PAGE, D), page_table.reshape(GROUPS, REQS_G, MAXP), row_request.reshape(GROUPS, GROUP_ROWS), row_position.reshape(GROUPS, GROUP_ROWS))).reshape(ROWS, D)
    stream = resid.astype(jnp.float32) + jnp.dot(attention, out_proj, preferred_element_type=jnp.float32)
    scale_row = lax.rsqrt(lax.optimization_barrier(jnp.mean(stream * stream, axis=1, keepdims=True)) + 1e-06)
    normed = (stream * scale_row * norm_gain[None, :]).astype(jnp.bfloat16)
    shared_hidden = (jax.nn.silu(jnp.dot(normed, shared_gate, preferred_element_type=jnp.float32)) * jnp.dot(normed, shared_up, preferred_element_type=jnp.float32)).astype(jnp.bfloat16)
    shared_out = jnp.dot(shared_hidden, shared_down, preferred_element_type=jnp.float32)
    shared_scale = jax.nn.sigmoid(jnp.dot(normed, shared_scalar, preferred_element_type=jnp.float32))
    entries = ROWS * TOPK
    flat_expert = route_expert.reshape(-1)
    flat_row = jnp.arange(entries, dtype=jnp.int32) // TOPK
    flat_gate = route_gate.reshape(-1)
    order = jnp.argsort(flat_expert, stable=True).astype(jnp.int32)
    expert_ids = jnp.arange(EXPERTS, dtype=jnp.int32)
    counts = lax.optimization_barrier(jnp.sum((flat_expert[:, None] == expert_ids[None, :]).astype(jnp.int32), axis=0))
    starts = jnp.cumsum(counts) - counts
    limit = SLOTS * CAP

    def one_expert(total, expert):
        offsets = jnp.arange(limit, dtype=jnp.int32)
        picked = order[jnp.minimum(starts[expert] + offsets, entries - 1)]
        valid = offsets < counts[expert]
        holder = jnp.argmax(slot_expert == expert)
        rows = normed[flat_row[picked]]
        result = expert_block(rows, expert_gate[holder], expert_up[holder], expert_down[holder])
        term = jnp.where(valid[:, None], result.astype(jnp.float32) * flat_gate[picked][:, None], 0.0)
        return (total.at[flat_row[picked]].add(term), None)
    routed, _ = lax.scan(one_expert, jnp.zeros((ROWS, D), jnp.float32), expert_ids)
    return (stream + shared_scale[:, None] * shared_out + routed).astype(jnp.bfloat16)
```

```python
import jax
import jax.numpy as jnp
from jax import lax
from jax.sharding import PartitionSpec as P

HEADS = 16
HEAD_DIM = 128
TOPK = 4


def expert_block(rows, gate_w, up_w, down_w):
    gate = jnp.dot(rows, gate_w, preferred_element_type=jnp.float32)
    upper = jnp.dot(rows, up_w, preferred_element_type=jnp.float32)
    hidden = (jax.nn.silu(gate) * upper).astype(jnp.bfloat16)
    return jnp.dot(hidden, down_w, preferred_element_type=jnp.float32).astype(jnp.bfloat16)


def rms_normed(stream, norm_gain):
    scale_row = lax.rsqrt(jnp.mean(stream * stream, axis=1, keepdims=True) + 1e-06)
    return (stream * scale_row * norm_gain[None, :]).astype(jnp.bfloat16)


def gather_exp(piece, count):
    spread = jnp.broadcast_to(piece[None], (count,) + piece.shape)
    got = lax.all_to_all(spread, "exp", 0, 0, tiled=True)
    return got.reshape((count * piece.shape[0],) + piece.shape[1:])


def shards(
    resid,
    queries,
    cache_key,
    cache_value,
    page_table,
    row_request,
    row_position,
    out_proj,
    norm_gain,
    expert_gate,
    expert_up,
    expert_down,
    shared_gate,
    shared_up,
    shared_down,
    shared_scalar,
    slot_expert,
    route_expert,
    route_gate,
):
    exp_count = lax.axis_size("exp")
    req_count = lax.axis_size("req")
    slot_count = exp_count * req_count
    exp_index = lax.axis_index("exp")
    own_slot = lax.axis_index("req") * exp_count + exp_index
    tok_rows = resid.shape[0]
    model_width = resid.shape[1]
    group_rows = row_request.shape[0]
    pages_here = cache_key.shape[0]
    page_len = cache_key.shape[1]
    req_slots = page_table.shape[0]
    max_pages = page_table.shape[1]
    capacity = 3 * tok_rows * TOPK // slot_count

    whole_proj = lax.all_gather(out_proj, "exp", axis=0, tiled=True)

    whole_queries = gather_exp(queries, exp_count)
    page_ids = exp_index * pages_here + jnp.arange(pages_here, dtype=jnp.int32)
    hits = (page_table[None, :, :] == page_ids[:, None, None]).astype(jnp.int32)
    page_request = jnp.sum(
        hits * jnp.arange(req_slots, dtype=jnp.int32)[None, :, None], axis=(1, 2)
    )
    page_slot = jnp.sum(hits * jnp.arange(max_pages, dtype=jnp.int32)[None, None, :], axis=(1, 2))
    key_position = (
        page_slot[:, None] * page_len + jnp.arange(page_len, dtype=jnp.int32)[None, :]
    ).reshape(-1)
    key_request = jnp.repeat(page_request, page_len)
    visible = (row_request[:, None] == key_request[None, :]) & (
        key_position[None, :] <= row_position[:, None]
    )
    key_count = pages_here * page_len
    query_heads = whole_queries.reshape(group_rows, HEADS, HEAD_DIM)
    key_heads = cache_key.reshape(key_count, HEADS, HEAD_DIM)
    value_heads = cache_value.reshape(key_count, HEADS, HEAD_DIM)
    scores = jnp.einsum(
        "rhd,khd->hrk", query_heads, key_heads, preferred_element_type=jnp.float32
    ) * HEAD_DIM ** (-0.5)
    scores = jnp.where(visible[None], scores, -1e30)
    local_top = jnp.max(scores, axis=2)
    weights = jnp.where(visible[None], jnp.exp(scores - local_top[:, :, None]), 0.0)
    local_den = jnp.sum(weights, axis=2)
    numerators = jnp.einsum(
        "hrk,khd->rhd",
        weights.astype(jnp.bfloat16),
        value_heads,
        preferred_element_type=jnp.float32,
    ).reshape(exp_count, tok_rows, model_width)
    stats = jnp.concatenate(
        [jnp.transpose(local_top), jnp.transpose(local_den)], axis=1
    ).reshape(exp_count, tok_rows, 2 * HEADS)
    got_num = lax.all_to_all(numerators.astype(jnp.bfloat16), "exp", 0, 0, tiled=True)
    got_stats = lax.all_to_all(stats, "exp", 0, 0, tiled=True)
    part_top = got_stats[:, :, :HEADS]
    part_den = got_stats[:, :, HEADS:]
    top = jnp.max(part_top, axis=0)
    shift = jnp.exp(part_top - top[None])
    denominators = jnp.sum(shift * part_den, axis=0)
    combined = jnp.sum(
        got_num.astype(jnp.float32).reshape(exp_count, tok_rows, HEADS, HEAD_DIM)
        * shift[:, :, :, None],
        axis=0,
    )
    attention = (
        (combined / denominators[:, :, None]).reshape(tok_rows, model_width).astype(jnp.bfloat16)
    )
    mixed = jnp.dot(attention, whole_proj, preferred_element_type=jnp.float32)
    stream = resid.astype(jnp.float32) + mixed
    normed = rms_normed(stream, norm_gain)

    piece = gather_exp(normed, exp_count)
    gate = jnp.dot(piece, shared_gate, preferred_element_type=jnp.float32)
    upper = jnp.dot(piece, shared_up, preferred_element_type=jnp.float32)
    shared_hidden = (jax.nn.silu(gate) * upper).astype(jnp.bfloat16)
    shared_part = jnp.dot(
        shared_hidden, shared_down, preferred_element_type=jnp.float32
    ).astype(jnp.bfloat16)
    shared_out = jnp.sum(
        lax.all_to_all(
            shared_part.reshape(exp_count, tok_rows, model_width), "exp", 0, 0, tiled=True
        ).astype(jnp.float32),
        axis=0,
    )
    shared_scale = jax.nn.sigmoid(
        jnp.dot(normed, shared_scalar, preferred_element_type=jnp.float32)
    )

    slot_ids = jnp.arange(slot_count, dtype=jnp.int32)
    same_expert = slot_expert[:, None] == slot_expert[None, :]
    copy_rank = jnp.sum(
        (same_expert & (slot_ids[None, :] < slot_ids[:, None])).astype(jnp.int32), axis=1
    )
    own_routes = lax.dynamic_slice_in_dim(route_expert, own_slot * tok_rows, tok_rows, 0).reshape(
        -1
    )
    holds = own_routes[:, None] == slot_expert[None, :]
    chosen = holds & (copy_rank[None, :] == 0)
    target = jnp.sum(jnp.where(chosen, slot_ids[None, :], 0), axis=1)
    onehot = chosen.astype(jnp.int32)
    position = jnp.sum(jnp.cumsum(onehot, axis=0) * onehot, axis=1) - 1
    buffer_index = target * capacity + position
    entry_rows = jnp.repeat(normed, TOPK, axis=0)
    outgoing = (
        jnp.zeros((slot_count * capacity, model_width), jnp.bfloat16)
        .at[buffer_index]
        .set(entry_rows)
    )
    outgoing = outgoing.reshape(slot_count, capacity, model_width)
    incoming = lax.all_to_all(outgoing, ("req", "exp"), split_axis=0, concat_axis=0, tiled=True)
    answered = expert_block(
        incoming.reshape(-1, model_width), expert_gate[0], expert_up[0], expert_down[0]
    ).reshape(slot_count, capacity, model_width)
    returned = lax.all_to_all(
        answered, ("req", "exp"), split_axis=0, concat_axis=0, tiled=True
    ).reshape(-1, model_width)
    expert_out = returned[buffer_index].reshape(tok_rows, TOPK, model_width)
    routed = jnp.sum(expert_out.astype(jnp.float32) * route_gate[:, :, None], axis=1)
    return (stream + shared_scale[:, None] * shared_out + routed).astype(jnp.bfloat16)


def solution(mesh):
    placed = (
        P(("req", "exp"), None),
        P(("req", "exp"), None),
        P(("req", "exp"), None, None),
        P(("req", "exp"), None, None),
        P("req", None),
        P("req"),
        P("req"),
        P("exp", None),
        P(),
        P(("req", "exp"), None, None),
        P(("req", "exp"), None, None),
        P(("req", "exp"), None, None),
        P(None, "exp"),
        P(None, "exp"),
        P("exp", None),
        P(),
        P(),
        P(),
        P(("req", "exp"), None),
    )
    return jax.shard_map(
        shards, mesh=mesh, in_specs=placed, out_specs=P(("req", "exp"), None), check_vma=False
    )
```

```python
import jax
import jax.numpy as jnp
from jax import lax
from jax.sharding import PartitionSpec as P

HEADS = 16
HEAD_DIM = 128
TOPK = 4


def expert_block(rows, gate_w, up_w, down_w):
    gate = jnp.dot(rows, gate_w, preferred_element_type=jnp.float32)
    upper = jnp.dot(rows, up_w, preferred_element_type=jnp.float32)
    hidden = (jax.nn.silu(gate) * upper).astype(jnp.bfloat16)
    return jnp.dot(hidden, down_w, preferred_element_type=jnp.float32).astype(jnp.bfloat16)


def rms_normed(stream, norm_gain):
    scale_row = lax.rsqrt(jnp.mean(stream * stream, axis=1, keepdims=True) + 1e-06)
    return (stream * scale_row * norm_gain[None, :]).astype(jnp.bfloat16)


def gather_exp(piece, count):
    spread = jnp.broadcast_to(piece[None], (count,) + piece.shape)
    got = lax.all_to_all(spread, "exp", 0, 0, tiled=True)
    return got.reshape((count * piece.shape[0],) + piece.shape[1:])


def shards(
    resid,
    queries,
    cache_key,
    cache_value,
    page_table,
    row_request,
    row_position,
    out_proj,
    norm_gain,
    expert_gate,
    expert_up,
    expert_down,
    shared_gate,
    shared_up,
    shared_down,
    shared_scalar,
    slot_expert,
    route_expert,
    route_gate,
):
    exp_count = lax.axis_size("exp")
    req_count = lax.axis_size("req")
    slot_count = exp_count * req_count
    exp_index = lax.axis_index("exp")
    own_slot = lax.axis_index("req") * exp_count + exp_index
    tok_rows = resid.shape[0]
    model_width = resid.shape[1]
    group_rows = row_request.shape[0]
    pages_here = cache_key.shape[0]
    page_len = cache_key.shape[1]
    req_slots = page_table.shape[0]
    max_pages = page_table.shape[1]
    capacity = 3 * tok_rows * TOPK // slot_count

    query_cols = lax.all_to_all(
        queries.reshape(tok_rows, HEADS, HEAD_DIM).transpose(1, 0, 2), "exp", 0, 0, tiled=True
    ).reshape(group_rows, HEAD_DIM)
    key_count = pages_here * page_len
    group_keys = exp_count * key_count
    key_cols = lax.all_to_all(
        cache_key.reshape(key_count, HEADS, HEAD_DIM).transpose(1, 0, 2), "exp", 0, 0, tiled=True
    ).reshape(group_keys, HEAD_DIM)
    value_cols = lax.all_to_all(
        cache_value.reshape(key_count, HEADS, HEAD_DIM).transpose(1, 0, 2), "exp", 0, 0, tiled=True
    ).reshape(group_keys, HEAD_DIM)
    page_ids = jnp.arange(exp_count * pages_here, dtype=jnp.int32)
    hits = (page_table[None, :, :] == page_ids[:, None, None]).astype(jnp.int32)
    page_request = jnp.sum(
        hits * jnp.arange(req_slots, dtype=jnp.int32)[None, :, None], axis=(1, 2)
    )
    page_slot = jnp.sum(hits * jnp.arange(max_pages, dtype=jnp.int32)[None, None, :], axis=(1, 2))
    key_position = (
        page_slot[:, None] * page_len + jnp.arange(page_len, dtype=jnp.int32)[None, :]
    ).reshape(-1)
    key_request = jnp.repeat(page_request, page_len)
    visible = (row_request[:, None] == key_request[None, :]) & (
        key_position[None, :] <= row_position[:, None]
    )
    scores = jnp.dot(
        query_cols, key_cols.T, preferred_element_type=jnp.float32
    ) * HEAD_DIM ** (-0.5)
    scores = jnp.where(visible, scores, -1e30)
    top = jnp.max(scores, axis=1)
    weights = jnp.where(visible, jnp.exp(scores - top[:, None]), 0.0)
    denominators = jnp.sum(weights, axis=1)
    numerators = jnp.dot(
        weights.astype(jnp.bfloat16), value_cols, preferred_element_type=jnp.float32
    )
    attention = (numerators / denominators[:, None]).astype(jnp.bfloat16)
    mixed_part = jnp.dot(attention, out_proj, preferred_element_type=jnp.float32)
    mixed = jnp.sum(
        lax.all_to_all(
            mixed_part.astype(jnp.bfloat16).reshape(exp_count, tok_rows, model_width),
            "exp", 0, 0, tiled=True,
        ).astype(jnp.float32),
        axis=0,
    )
    stream = resid.astype(jnp.float32) + mixed
    normed = rms_normed(stream, norm_gain)

    piece = gather_exp(normed, exp_count)
    gate = jnp.dot(piece, shared_gate, preferred_element_type=jnp.float32)
    upper = jnp.dot(piece, shared_up, preferred_element_type=jnp.float32)
    shared_hidden = (jax.nn.silu(gate) * upper).astype(jnp.bfloat16)
    shared_part = jnp.dot(
        shared_hidden, shared_down, preferred_element_type=jnp.float32
    ).astype(jnp.bfloat16)
    shared_out = jnp.sum(
        lax.all_to_all(
            shared_part.reshape(exp_count, tok_rows, model_width), "exp", 0, 0, tiled=True
        ).astype(jnp.float32),
        axis=0,
    )
    shared_scale = jax.nn.sigmoid(
        jnp.dot(normed, shared_scalar, preferred_element_type=jnp.float32)
    )

    slot_ids = jnp.arange(slot_count, dtype=jnp.int32)
    same_expert = slot_expert[:, None] == slot_expert[None, :]
    copy_rank = jnp.sum(
        (same_expert & (slot_ids[None, :] < slot_ids[:, None])).astype(jnp.int32), axis=1
    )
    own_routes = lax.dynamic_slice_in_dim(route_expert, own_slot * tok_rows, tok_rows, 0).reshape(
        -1
    )
    holds = own_routes[:, None] == slot_expert[None, :]
    chosen = holds & (copy_rank[None, :] == 0)
    target = jnp.sum(jnp.where(chosen, slot_ids[None, :], 0), axis=1)
    onehot = chosen.astype(jnp.int32)
    position = jnp.sum(jnp.cumsum(onehot, axis=0) * onehot, axis=1) - 1
    buffer_index = target * capacity + position
    entry_rows = jnp.repeat(normed, TOPK, axis=0)
    outgoing = (
        jnp.zeros((slot_count * capacity, model_width), jnp.bfloat16)
        .at[buffer_index]
        .set(entry_rows)
    )
    outgoing = outgoing.reshape(slot_count, capacity, model_width)
    incoming = lax.all_to_all(outgoing, ("req", "exp"), split_axis=0, concat_axis=0, tiled=True)
    answered = expert_block(
        incoming.reshape(-1, model_width), expert_gate[0], expert_up[0], expert_down[0]
    ).reshape(slot_count, capacity, model_width)
    returned = lax.all_to_all(
        answered, ("req", "exp"), split_axis=0, concat_axis=0, tiled=True
    ).reshape(-1, model_width)
    expert_out = returned[buffer_index].reshape(tok_rows, TOPK, model_width)
    routed = jnp.sum(expert_out.astype(jnp.float32) * route_gate[:, :, None], axis=1)
    return (stream + shared_scale[:, None] * shared_out + routed).astype(jnp.bfloat16)


def solution(mesh):
    placed = (
        P(("req", "exp"), None),
        P(("req", "exp"), None),
        P(("req", "exp"), None, None),
        P(("req", "exp"), None, None),
        P("req", None),
        P("req"),
        P("req"),
        P("exp", None),
        P(),
        P(("req", "exp"), None, None),
        P(("req", "exp"), None, None),
        P(("req", "exp"), None, None),
        P(None, "exp"),
        P(None, "exp"),
        P("exp", None),
        P(),
        P(),
        P(),
        P(("req", "exp"), None),
    )
    return jax.shard_map(
        shards, mesh=mesh, in_specs=placed, out_specs=P(("req", "exp"), None), check_vma=False
    )
```

```python
import jax
import jax.numpy as jnp
from jax import lax
from jax.sharding import PartitionSpec as P

HEADS = 16
HEAD_DIM = 128
TOPK = 4


def expert_block(rows, gate_w, up_w, down_w):
    gate = jnp.dot(rows, gate_w, preferred_element_type=jnp.float32)
    upper = jnp.dot(rows, up_w, preferred_element_type=jnp.float32)
    hidden = (jax.nn.silu(gate) * upper).astype(jnp.bfloat16)
    return jnp.dot(hidden, down_w, preferred_element_type=jnp.float32).astype(jnp.bfloat16)


def rms_normed(stream, norm_gain):
    scale_row = lax.rsqrt(jnp.mean(stream * stream, axis=1, keepdims=True) + 1e-06)
    return (stream * scale_row * norm_gain[None, :]).astype(jnp.bfloat16)


def gather_exp(piece, count):
    spread = jnp.broadcast_to(piece[None], (count,) + piece.shape)
    got = lax.all_to_all(spread, "exp", 0, 0, tiled=True)
    return got.reshape((count * piece.shape[0],) + piece.shape[1:])


def shards(
    resid,
    queries,
    cache_key,
    cache_value,
    page_table,
    row_request,
    row_position,
    out_proj,
    norm_gain,
    expert_gate,
    expert_up,
    expert_down,
    shared_gate,
    shared_up,
    shared_down,
    shared_scalar,
    slot_expert,
    route_expert,
    route_gate,
):
    exp_count = lax.axis_size("exp")
    req_count = lax.axis_size("req")
    slot_count = exp_count * req_count
    exp_index = lax.axis_index("exp")
    own_slot = lax.axis_index("req") * exp_count + exp_index
    tok_rows = resid.shape[0]
    model_width = resid.shape[1]
    group_rows = row_request.shape[0]
    pages_here = cache_key.shape[0]
    page_len = cache_key.shape[1]
    req_slots = page_table.shape[0]
    max_pages = page_table.shape[1]
    capacity = 3 * tok_rows * TOPK // slot_count

    key_count = pages_here * page_len
    group_keys = exp_count * key_count
    by_head = jnp.concatenate(
        [
            queries.reshape(tok_rows, HEADS, HEAD_DIM).transpose(1, 0, 2),
            cache_key.reshape(key_count, HEADS, HEAD_DIM).transpose(1, 0, 2),
            cache_value.reshape(key_count, HEADS, HEAD_DIM).transpose(1, 0, 2),
        ],
        axis=1,
    )
    got_cols = lax.all_to_all(by_head, "exp", 0, 0, tiled=True)
    query_cols = got_cols[:, :tok_rows].reshape(group_rows, HEAD_DIM)
    key_cols = got_cols[:, tok_rows:tok_rows + key_count].reshape(group_keys, HEAD_DIM)
    value_cols = got_cols[:, tok_rows + key_count:].reshape(group_keys, HEAD_DIM)
    page_ids = jnp.arange(exp_count * pages_here, dtype=jnp.int32)
    hits = (page_table[None, :, :] == page_ids[:, None, None]).astype(jnp.int32)
    page_request = jnp.sum(
        hits * jnp.arange(req_slots, dtype=jnp.int32)[None, :, None], axis=(1, 2)
    )
    page_slot = jnp.sum(hits * jnp.arange(max_pages, dtype=jnp.int32)[None, None, :], axis=(1, 2))
    key_position = (
        page_slot[:, None] * page_len + jnp.arange(page_len, dtype=jnp.int32)[None, :]
    ).reshape(-1)
    key_request = jnp.repeat(page_request, page_len)
    visible = (row_request[:, None] == key_request[None, :]) & (
        key_position[None, :] <= row_position[:, None]
    )
    scores = jnp.dot(
        query_cols, key_cols.T, preferred_element_type=jnp.float32
    ) * HEAD_DIM ** (-0.5)
    scores = jnp.where(visible, scores, -1e30)
    top = jnp.max(scores, axis=1)
    weights = jnp.where(visible, jnp.exp(scores - top[:, None]), 0.0)
    denominators = jnp.sum(weights, axis=1)
    numerators = jnp.dot(
        weights.astype(jnp.bfloat16), value_cols, preferred_element_type=jnp.float32
    )
    attention = (numerators / denominators[:, None]).astype(jnp.bfloat16)
    mixed_part = jnp.dot(attention, out_proj, preferred_element_type=jnp.float32)
    mixed = jnp.sum(
        lax.all_to_all(
            mixed_part.astype(jnp.bfloat16).reshape(exp_count, tok_rows, model_width),
            "exp", 0, 0, tiled=True,
        ).astype(jnp.float32),
        axis=0,
    )
    stream = resid.astype(jnp.float32) + mixed
    normed = rms_normed(stream, norm_gain)

    piece = gather_exp(normed, exp_count)
    gate = jnp.dot(piece, shared_gate, preferred_element_type=jnp.float32)
    upper = jnp.dot(piece, shared_up, preferred_element_type=jnp.float32)
    shared_hidden = (jax.nn.silu(gate) * upper).astype(jnp.bfloat16)
    shared_part = jnp.dot(
        shared_hidden, shared_down, preferred_element_type=jnp.float32
    ).astype(jnp.bfloat16)
    shared_out = jnp.sum(
        lax.all_to_all(
            shared_part.reshape(exp_count, tok_rows, model_width), "exp", 0, 0, tiled=True
        ).astype(jnp.float32),
        axis=0,
    )
    shared_scale = jax.nn.sigmoid(
        jnp.dot(normed, shared_scalar, preferred_element_type=jnp.float32)
    )

    slot_ids = jnp.arange(slot_count, dtype=jnp.int32)
    same_expert = slot_expert[:, None] == slot_expert[None, :]
    copy_rank = jnp.sum(
        (same_expert & (slot_ids[None, :] < slot_ids[:, None])).astype(jnp.int32), axis=1
    )
    own_routes = lax.dynamic_slice_in_dim(route_expert, own_slot * tok_rows, tok_rows, 0).reshape(
        -1
    )
    holds = own_routes[:, None] == slot_expert[None, :]
    chosen = holds & (copy_rank[None, :] == 0)
    target = jnp.sum(jnp.where(chosen, slot_ids[None, :], 0), axis=1)
    onehot = chosen.astype(jnp.int32)
    position = jnp.sum(jnp.cumsum(onehot, axis=0) * onehot, axis=1) - 1
    entry_rows = jnp.repeat(normed, TOPK, axis=0)
    outgoing = (
        jnp.zeros((slot_count, capacity, model_width), jnp.bfloat16)
        .at[target, position]
        .set(entry_rows)
    )
    incoming = lax.all_to_all(outgoing, ("req", "exp"), split_axis=0, concat_axis=0, tiled=True)
    answered = expert_block(incoming, expert_gate[0], expert_up[0], expert_down[0])
    returned = lax.all_to_all(
        answered, ("req", "exp"), split_axis=0, concat_axis=0, tiled=True
    )
    expert_out = returned[target, position].reshape(tok_rows, TOPK, model_width)
    routed = jnp.sum(expert_out.astype(jnp.float32) * route_gate[:, :, None], axis=1)
    return (stream + shared_scale[:, None] * shared_out + routed).astype(jnp.bfloat16)


def solution(mesh):
    placed = (
        P(("req", "exp"), None),
        P(("req", "exp"), None),
        P(("req", "exp"), None, None),
        P(("req", "exp"), None, None),
        P("req", None),
        P("req"),
        P("req"),
        P("exp", None),
        P(),
        P(("req", "exp"), None, None),
        P(("req", "exp"), None, None),
        P(("req", "exp"), None, None),
        P(None, "exp"),
        P(None, "exp"),
        P("exp", None),
        P(),
        P(),
        P(),
        P(("req", "exp"), None),
    )
    return jax.shard_map(
        shards, mesh=mesh, in_specs=placed, out_specs=P(("req", "exp"), None), check_vma=False
    )
```

```python
import jax
import jax.numpy as jnp
from jax import lax
from jax.sharding import PartitionSpec as P

HEADS = 16
HEAD_DIM = 128
TOPK = 4


def expert_block(rows, gate_w, up_w, down_w):
    gate = jnp.dot(rows, gate_w, preferred_element_type=jnp.float32)
    upper = jnp.dot(rows, up_w, preferred_element_type=jnp.float32)
    hidden = (jax.nn.silu(gate) * upper).astype(jnp.bfloat16)
    return jnp.dot(hidden, down_w, preferred_element_type=jnp.float32).astype(jnp.bfloat16)


def rms_normed(stream, norm_gain):
    scale_row = lax.rsqrt(jnp.mean(stream * stream, axis=1, keepdims=True) + 1e-06)
    return (stream * scale_row * norm_gain[None, :]).astype(jnp.bfloat16)


def gather_exp(piece, count):
    spread = jnp.broadcast_to(piece[None], (count,) + piece.shape)
    got = lax.all_to_all(spread, "exp", 0, 0, tiled=True)
    return got.reshape((count * piece.shape[0],) + piece.shape[1:])


def shards(
    resid,
    queries,
    cache_key,
    cache_value,
    page_table,
    row_request,
    row_position,
    out_proj,
    norm_gain,
    expert_gate,
    expert_up,
    expert_down,
    shared_gate,
    shared_up,
    shared_down,
    shared_scalar,
    slot_expert,
    route_expert,
    route_gate,
):
    exp_count = lax.axis_size("exp")
    req_count = lax.axis_size("req")
    slot_count = exp_count * req_count
    exp_index = lax.axis_index("exp")
    own_slot = lax.axis_index("req") * exp_count + exp_index
    tok_rows = resid.shape[0]
    model_width = resid.shape[1]
    group_rows = row_request.shape[0]
    pages_here = cache_key.shape[0]
    page_len = cache_key.shape[1]
    req_slots = page_table.shape[0]
    max_pages = page_table.shape[1]
    capacity = 3 * tok_rows * TOPK // slot_count

    key_count = pages_here * page_len
    group_keys = exp_count * key_count
    by_head = jnp.concatenate(
        [
            queries.reshape(tok_rows, HEADS, HEAD_DIM).transpose(1, 0, 2),
            cache_key.reshape(key_count, HEADS, HEAD_DIM).transpose(1, 0, 2),
            cache_value.reshape(key_count, HEADS, HEAD_DIM).transpose(1, 0, 2),
        ],
        axis=1,
    )
    got_cols = lax.all_to_all(by_head, "exp", 0, 0, tiled=True)
    query_cols = got_cols[:, :tok_rows].reshape(group_rows, HEAD_DIM)
    key_cols = got_cols[:, tok_rows:tok_rows + key_count].reshape(group_keys, HEAD_DIM)
    value_cols = got_cols[:, tok_rows + key_count:].reshape(group_keys, HEAD_DIM)
    page_ids = jnp.arange(exp_count * pages_here, dtype=jnp.int32)
    hits = (page_table[None, :, :] == page_ids[:, None, None]).astype(jnp.int32)
    page_request = jnp.sum(
        hits * jnp.arange(req_slots, dtype=jnp.int32)[None, :, None], axis=(1, 2)
    )
    page_slot = jnp.sum(hits * jnp.arange(max_pages, dtype=jnp.int32)[None, None, :], axis=(1, 2))
    key_position = (
        page_slot[:, None] * page_len + jnp.arange(page_len, dtype=jnp.int32)[None, :]
    ).reshape(-1)
    key_request = jnp.repeat(page_request, page_len)
    visible = (row_request[:, None] == key_request[None, :]) & (
        key_position[None, :] <= row_position[:, None]
    )
    scores = jnp.dot(
        query_cols, key_cols.T, preferred_element_type=jnp.float32
    ) * HEAD_DIM ** (-0.5)
    scores = jnp.where(visible, scores, -1e30)
    top = jnp.max(scores, axis=1)
    weights = jnp.where(visible, jnp.exp(scores - top[:, None]), 0.0)
    denominators = jnp.sum(weights, axis=1)
    numerators = jnp.dot(
        weights.astype(jnp.bfloat16), value_cols, preferred_element_type=jnp.float32
    )
    attention = (numerators / denominators[:, None]).astype(jnp.bfloat16)
    mixed_part = jnp.dot(attention, out_proj, preferred_element_type=jnp.float32)
    mixed = jnp.sum(
        lax.all_to_all(
            mixed_part.astype(jnp.bfloat16).reshape(exp_count, tok_rows, model_width),
            "exp", 0, 0, tiled=True,
        ).astype(jnp.float32),
        axis=0,
    )
    stream = resid.astype(jnp.float32) + mixed
    normed = rms_normed(stream, norm_gain)

    piece = gather_exp(normed, exp_count)
    gate = jnp.dot(piece, shared_gate, preferred_element_type=jnp.float32)
    upper = jnp.dot(piece, shared_up, preferred_element_type=jnp.float32)
    shared_hidden = (jax.nn.silu(gate) * upper).astype(jnp.bfloat16)
    shared_part = jnp.dot(
        shared_hidden, shared_down, preferred_element_type=jnp.float32
    ).astype(jnp.bfloat16)
    shared_out = jnp.sum(
        lax.all_to_all(
            shared_part.reshape(exp_count, tok_rows, model_width), "exp", 0, 0, tiled=True
        ).astype(jnp.float32),
        axis=0,
    )
    shared_scale = jax.nn.sigmoid(
        jnp.dot(normed, shared_scalar, preferred_element_type=jnp.float32)
    )

    slot_ids = jnp.arange(slot_count, dtype=jnp.int32)
    same_expert = slot_expert[:, None] == slot_expert[None, :]
    copy_rank = jnp.sum(
        (same_expert & (slot_ids[None, :] < slot_ids[:, None])).astype(jnp.int32), axis=1
    )
    own_routes = lax.dynamic_slice_in_dim(route_expert, own_slot * tok_rows, tok_rows, 0).reshape(
        -1
    )
    holds = own_routes[:, None] == slot_expert[None, :]
    chosen = holds & (copy_rank[None, :] == 0)
    target = jnp.sum(jnp.where(chosen, slot_ids[None, :], 0), axis=1)
    onehot = chosen.astype(jnp.int32)
    position = jnp.sum(jnp.cumsum(onehot, axis=0) * onehot, axis=1) - 1
    buffer_index = target * capacity + position
    entry_rows = jnp.repeat(normed, TOPK, axis=0)
    outgoing = (
        jnp.zeros((slot_count * capacity, model_width), jnp.bfloat16)
        .at[buffer_index]
        .set(entry_rows)
    )
    outgoing = outgoing.reshape(slot_count, capacity, model_width)
    incoming = lax.all_to_all(outgoing, ("req", "exp"), split_axis=0, concat_axis=0, tiled=True)
    answered = expert_block(
        incoming.reshape(-1, model_width), expert_gate[0], expert_up[0], expert_down[0]
    ).reshape(slot_count, capacity, model_width)
    returned = lax.all_to_all(
        answered, ("req", "exp"), split_axis=0, concat_axis=0, tiled=True
    ).reshape(-1, model_width)
    expert_out = returned[buffer_index].reshape(tok_rows, TOPK, model_width)
    routed = jnp.sum(expert_out.astype(jnp.float32) * route_gate[:, :, None], axis=1)
    return (stream + shared_scale[:, None] * shared_out + routed).astype(jnp.bfloat16)


def solution(mesh):
    placed = (
        P(("req", "exp"), None),
        P(("req", "exp"), None),
        P(("req", "exp"), None, None),
        P(("req", "exp"), None, None),
        P("req", None),
        P("req"),
        P("req"),
        P("exp", None),
        P(),
        P(("req", "exp"), None, None),
        P(("req", "exp"), None, None),
        P(("req", "exp"), None, None),
        P(None, "exp"),
        P(None, "exp"),
        P("exp", None),
        P(),
        P(),
        P(),
        P(("req", "exp"), None),
    )
    return jax.shard_map(
        shards, mesh=mesh, in_specs=placed, out_specs=P(("req", "exp"), None), check_vma=False
    )
```

```python
import jax
import jax.numpy as jnp
from jax import lax
from jax.experimental import pallas as pl
from jax.sharding import PartitionSpec as P

HEADS = 16
HEAD_DIM = 128
TOPK = 4


def expert_block(rows, gate_w, up_w, down_w):
    gate = jnp.dot(rows, gate_w, preferred_element_type=jnp.float32)
    upper = jnp.dot(rows, up_w, preferred_element_type=jnp.float32)
    hidden = (jax.nn.silu(gate) * upper).astype(jnp.bfloat16)
    return jnp.dot(hidden, down_w, preferred_element_type=jnp.float32).astype(jnp.bfloat16)


def rms_normed(stream, norm_gain):
    scale_row = lax.rsqrt(jnp.mean(stream * stream, axis=1, keepdims=True) + 1e-06)
    return (stream * scale_row * norm_gain[None, :]).astype(jnp.bfloat16)


def head_attention_kernel(q_ref, k_ref, v_ref, rreq_ref, rpos_ref, kreq_ref, kpos_ref, o_ref):
    scores = lax.dot_general(
        q_ref[...], k_ref[...], (((1,), (1,)), ((), ())), preferred_element_type=jnp.float32
    ) * HEAD_DIM ** (-0.5)
    visible = (rreq_ref[...] == kreq_ref[...]) & (kpos_ref[...] <= rpos_ref[...])
    scores = jnp.where(visible, scores, -1e30)
    top = jnp.max(scores, axis=1, keepdims=True)
    weights = jnp.where(visible, jnp.exp(scores - top), 0.0)
    denominators = jnp.sum(weights, axis=1, keepdims=True)
    numerators = jnp.dot(
        weights.astype(jnp.bfloat16), v_ref[...], preferred_element_type=jnp.float32
    )
    o_ref[...] = (numerators / denominators).astype(o_ref.dtype)


def head_attention(query_cols, key_cols, value_cols, row_request, row_position, key_request, key_position):
    rows, width = query_cols.shape
    keys = key_cols.shape[0]
    tile = 128
    row_spec = pl.BlockSpec((tile, width), lambda i: (i, 0))
    whole = pl.BlockSpec((keys, width), lambda i: (0, 0))
    row_int = pl.BlockSpec((tile, 1), lambda i: (i, 0))
    key_int = pl.BlockSpec((1, keys), lambda i: (0, 0))
    return pl.pallas_call(
        head_attention_kernel,
        grid=(rows // tile,),
        out_shape=jax.ShapeDtypeStruct((rows, width), jnp.bfloat16),
        in_specs=[row_spec, whole, whole, row_int, row_int, key_int, key_int],
        out_specs=row_spec,
        cost_estimate=pl.CostEstimate(
            flops=4 * rows * keys * width, transcendentals=rows * keys, bytes_accessed=3 * keys * width * 2
        ),
    )(
        query_cols,
        key_cols,
        value_cols,
        row_request.reshape(rows, 1),
        row_position.reshape(rows, 1),
        key_request.reshape(1, keys),
        key_position.reshape(1, keys),
    )


def gather_exp(piece, count):
    spread = jnp.broadcast_to(piece[None], (count,) + piece.shape)
    got = lax.all_to_all(spread, "exp", 0, 0, tiled=True)
    return got.reshape((count * piece.shape[0],) + piece.shape[1:])


def shards(
    resid,
    queries,
    cache_key,
    cache_value,
    page_table,
    row_request,
    row_position,
    out_proj,
    norm_gain,
    expert_gate,
    expert_up,
    expert_down,
    shared_gate,
    shared_up,
    shared_down,
    shared_scalar,
    slot_expert,
    route_expert,
    route_gate,
):
    exp_count = lax.axis_size("exp")
    req_count = lax.axis_size("req")
    slot_count = exp_count * req_count
    exp_index = lax.axis_index("exp")
    own_slot = lax.axis_index("req") * exp_count + exp_index
    tok_rows = resid.shape[0]
    model_width = resid.shape[1]
    group_rows = row_request.shape[0]
    pages_here = cache_key.shape[0]
    page_len = cache_key.shape[1]
    req_slots = page_table.shape[0]
    max_pages = page_table.shape[1]
    capacity = 3 * tok_rows * TOPK // slot_count

    key_count = pages_here * page_len
    group_keys = exp_count * key_count
    by_head = jnp.concatenate(
        [
            queries.reshape(tok_rows, HEADS, HEAD_DIM).transpose(1, 0, 2),
            cache_key.reshape(key_count, HEADS, HEAD_DIM).transpose(1, 0, 2),
            cache_value.reshape(key_count, HEADS, HEAD_DIM).transpose(1, 0, 2),
        ],
        axis=1,
    )
    got_cols = lax.all_to_all(by_head, "exp", 0, 0, tiled=True)
    query_cols = got_cols[:, :tok_rows].reshape(group_rows, HEAD_DIM)
    key_cols = got_cols[:, tok_rows:tok_rows + key_count].reshape(group_keys, HEAD_DIM)
    value_cols = got_cols[:, tok_rows + key_count:].reshape(group_keys, HEAD_DIM)
    page_ids = jnp.arange(exp_count * pages_here, dtype=jnp.int32)
    hits = (page_table[None, :, :] == page_ids[:, None, None]).astype(jnp.int32)
    page_request = jnp.sum(
        hits * jnp.arange(req_slots, dtype=jnp.int32)[None, :, None], axis=(1, 2)
    )
    page_slot = jnp.sum(hits * jnp.arange(max_pages, dtype=jnp.int32)[None, None, :], axis=(1, 2))
    key_position = (
        page_slot[:, None] * page_len + jnp.arange(page_len, dtype=jnp.int32)[None, :]
    ).reshape(-1)
    key_request = jnp.repeat(page_request, page_len)
    attention = head_attention(
        query_cols, key_cols, value_cols, row_request, row_position, key_request, key_position
    )
    mixed_part = jnp.dot(attention, out_proj, preferred_element_type=jnp.float32)
    mixed = jnp.sum(
        lax.all_to_all(
            mixed_part.astype(jnp.bfloat16).reshape(exp_count, tok_rows, model_width),
            "exp", 0, 0, tiled=True,
        ).astype(jnp.float32),
        axis=0,
    )
    stream = resid.astype(jnp.float32) + mixed
    normed = rms_normed(stream, norm_gain)

    piece = gather_exp(normed, exp_count)
    gate = jnp.dot(piece, shared_gate, preferred_element_type=jnp.float32)
    upper = jnp.dot(piece, shared_up, preferred_element_type=jnp.float32)
    shared_hidden = (jax.nn.silu(gate) * upper).astype(jnp.bfloat16)
    shared_part = jnp.dot(
        shared_hidden, shared_down, preferred_element_type=jnp.float32
    ).astype(jnp.bfloat16)
    shared_out = jnp.sum(
        lax.all_to_all(
            shared_part.reshape(exp_count, tok_rows, model_width), "exp", 0, 0, tiled=True
        ).astype(jnp.float32),
        axis=0,
    )
    shared_scale = jax.nn.sigmoid(
        jnp.dot(normed, shared_scalar, preferred_element_type=jnp.float32)
    )

    slot_ids = jnp.arange(slot_count, dtype=jnp.int32)
    same_expert = slot_expert[:, None] == slot_expert[None, :]
    copy_rank = jnp.sum(
        (same_expert & (slot_ids[None, :] < slot_ids[:, None])).astype(jnp.int32), axis=1
    )
    own_routes = lax.dynamic_slice_in_dim(route_expert, own_slot * tok_rows, tok_rows, 0).reshape(
        -1
    )
    holds = own_routes[:, None] == slot_expert[None, :]
    chosen = holds & (copy_rank[None, :] == 0)
    target = jnp.sum(jnp.where(chosen, slot_ids[None, :], 0), axis=1)
    onehot = chosen.astype(jnp.int32)
    position = jnp.sum(jnp.cumsum(onehot, axis=0) * onehot, axis=1) - 1
    buffer_index = target * capacity + position
    entry_rows = jnp.repeat(normed, TOPK, axis=0)
    outgoing = (
        jnp.zeros((slot_count * capacity, model_width), jnp.bfloat16)
        .at[buffer_index]
        .set(entry_rows)
    )
    outgoing = outgoing.reshape(slot_count, capacity, model_width)
    incoming = lax.all_to_all(outgoing, ("req", "exp"), split_axis=0, concat_axis=0, tiled=True)
    answered = expert_block(
        incoming.reshape(-1, model_width), expert_gate[0], expert_up[0], expert_down[0]
    ).reshape(slot_count, capacity, model_width)
    returned = lax.all_to_all(
        answered, ("req", "exp"), split_axis=0, concat_axis=0, tiled=True
    ).reshape(-1, model_width)
    expert_out = returned[buffer_index].reshape(tok_rows, TOPK, model_width)
    routed = jnp.sum(expert_out.astype(jnp.float32) * route_gate[:, :, None], axis=1)
    return (stream + shared_scale[:, None] * shared_out + routed).astype(jnp.bfloat16)


def solution(mesh):
    placed = (
        P(("req", "exp"), None),
        P(("req", "exp"), None),
        P(("req", "exp"), None, None),
        P(("req", "exp"), None, None),
        P("req", None),
        P("req"),
        P("req"),
        P("exp", None),
        P(),
        P(("req", "exp"), None, None),
        P(("req", "exp"), None, None),
        P(("req", "exp"), None, None),
        P(None, "exp"),
        P(None, "exp"),
        P("exp", None),
        P(),
        P(),
        P(),
        P(("req", "exp"), None),
    )
    return jax.shard_map(
        shards, mesh=mesh, in_specs=placed, out_specs=P(("req", "exp"), None), check_vma=False
    )
```

```python
import jax
import jax.numpy as jnp
from jax import lax
from jax.experimental import pallas as pl
from jax.sharding import PartitionSpec as P

HEADS = 16
HEAD_DIM = 128
TOPK = 4


def expert_block(rows, gate_w, up_w, down_w):
    gate = jnp.dot(rows, gate_w, preferred_element_type=jnp.float32)
    upper = jnp.dot(rows, up_w, preferred_element_type=jnp.float32)
    hidden = (jax.nn.silu(gate) * upper).astype(jnp.bfloat16)
    return jnp.dot(hidden, down_w, preferred_element_type=jnp.float32).astype(jnp.bfloat16)


def rms_normed(stream, norm_gain):
    scale_row = lax.rsqrt(jnp.mean(stream * stream, axis=1, keepdims=True) + 1e-06)
    return (stream * scale_row * norm_gain[None, :]).astype(jnp.bfloat16)


def head_attention_kernel(q_ref, k_ref, v_ref, rreq_ref, rpos_ref, kreq_ref, kpos_ref, o_ref):
    scores = lax.dot_general(
        q_ref[...], k_ref[...], (((1,), (1,)), ((), ())), preferred_element_type=jnp.float32
    ) * HEAD_DIM ** (-0.5)
    visible = (rreq_ref[...] == kreq_ref[...]) & (kpos_ref[...] <= rpos_ref[...])
    scores = jnp.where(visible, scores, -1e30)
    top = jnp.max(scores, axis=1, keepdims=True)
    weights = jnp.where(visible, jnp.exp(scores - top), 0.0)
    denominators = jnp.sum(weights, axis=1, keepdims=True)
    numerators = jnp.dot(
        weights.astype(jnp.bfloat16), v_ref[...], preferred_element_type=jnp.float32
    )
    o_ref[...] = (numerators / denominators).astype(o_ref.dtype)


def head_attention(query_cols, key_cols, value_cols, row_request, row_position, key_request, key_position):
    rows, width = query_cols.shape
    keys = key_cols.shape[0]
    tile = 128
    row_spec = pl.BlockSpec((tile, width), lambda i: (i, 0))
    whole = pl.BlockSpec((keys, width), lambda i: (0, 0))
    row_int = pl.BlockSpec((tile, 1), lambda i: (i, 0))
    key_int = pl.BlockSpec((1, keys), lambda i: (0, 0))
    return pl.pallas_call(
        head_attention_kernel,
        grid=(rows // tile,),
        out_shape=jax.ShapeDtypeStruct((rows, width), jnp.bfloat16),
        in_specs=[row_spec, whole, whole, row_int, row_int, key_int, key_int],
        out_specs=row_spec,
        cost_estimate=pl.CostEstimate(
            flops=4 * rows * keys * width, transcendentals=rows * keys, bytes_accessed=3 * keys * width * 2
        ),
    )(
        query_cols,
        key_cols,
        value_cols,
        row_request.reshape(rows, 1),
        row_position.reshape(rows, 1),
        key_request.reshape(1, keys),
        key_position.reshape(1, keys),
    )


def gather_exp(piece, count):
    spread = jnp.broadcast_to(piece[None], (count,) + piece.shape)
    got = lax.all_to_all(spread, "exp", 0, 0, tiled=True)
    return got.reshape((count * piece.shape[0],) + piece.shape[1:])


def shards(
    resid,
    queries,
    cache_key,
    cache_value,
    page_table,
    row_request,
    row_position,
    out_proj,
    norm_gain,
    expert_gate,
    expert_up,
    expert_down,
    shared_gate,
    shared_up,
    shared_down,
    shared_scalar,
    slot_expert,
    route_expert,
    route_gate,
):
    exp_count = lax.axis_size("exp")
    req_count = lax.axis_size("req")
    slot_count = exp_count * req_count
    exp_index = lax.axis_index("exp")
    own_slot = lax.axis_index("req") * exp_count + exp_index
    tok_rows = resid.shape[0]
    model_width = resid.shape[1]
    group_rows = row_request.shape[0]
    pages_here = cache_key.shape[0]
    page_len = cache_key.shape[1]
    req_slots = page_table.shape[0]
    max_pages = page_table.shape[1]
    capacity = 3 * tok_rows * TOPK // slot_count

    key_count = pages_here * page_len
    group_keys = exp_count * key_count
    by_head = jnp.concatenate(
        [
            queries.reshape(tok_rows, HEADS, HEAD_DIM).transpose(1, 0, 2),
            cache_key.reshape(key_count, HEADS, HEAD_DIM).transpose(1, 0, 2),
            cache_value.reshape(key_count, HEADS, HEAD_DIM).transpose(1, 0, 2),
        ],
        axis=1,
    )
    got_cols = lax.all_to_all(by_head, "exp", 0, 0, tiled=True)
    query_cols = got_cols[:, :tok_rows].reshape(group_rows, HEAD_DIM)
    key_cols = got_cols[:, tok_rows:tok_rows + key_count].reshape(group_keys, HEAD_DIM)
    value_cols = got_cols[:, tok_rows + key_count:].reshape(group_keys, HEAD_DIM)
    page_ids = jnp.arange(exp_count * pages_here, dtype=jnp.int32)
    hits = (page_table[None, :, :] == page_ids[:, None, None]).astype(jnp.int32)
    page_request = jnp.sum(
        hits * jnp.arange(req_slots, dtype=jnp.int32)[None, :, None], axis=(1, 2)
    )
    page_slot = jnp.sum(hits * jnp.arange(max_pages, dtype=jnp.int32)[None, None, :], axis=(1, 2))
    key_position = (
        page_slot[:, None] * page_len + jnp.arange(page_len, dtype=jnp.int32)[None, :]
    ).reshape(-1)
    key_request = jnp.repeat(page_request, page_len)
    attention = head_attention(
        query_cols, key_cols, value_cols, row_request, row_position, key_request, key_position
    )
    mixed_part = jnp.dot(attention, out_proj, preferred_element_type=jnp.float32)
    mixed = jnp.sum(
        lax.all_to_all(
            mixed_part.astype(jnp.bfloat16).reshape(exp_count, tok_rows, model_width),
            "exp", 0, 0, tiled=True,
        ).astype(jnp.float32),
        axis=0,
    )
    stream = resid.astype(jnp.float32) + mixed
    normed = rms_normed(stream, norm_gain)

    piece = lax.all_gather(normed, "exp", axis=0, tiled=True)
    gate = jnp.dot(piece, shared_gate, preferred_element_type=jnp.float32)
    upper = jnp.dot(piece, shared_up, preferred_element_type=jnp.float32)
    shared_hidden = (jax.nn.silu(gate) * upper).astype(jnp.bfloat16)
    shared_part = jnp.dot(
        shared_hidden, shared_down, preferred_element_type=jnp.float32
    ).astype(jnp.bfloat16)
    shared_out = lax.psum_scatter(
        shared_part, "exp", scatter_dimension=0, tiled=True
    ).astype(jnp.float32)
    shared_scale = jax.nn.sigmoid(
        jnp.dot(normed, shared_scalar, preferred_element_type=jnp.float32)
    )

    slot_ids = jnp.arange(slot_count, dtype=jnp.int32)
    same_expert = slot_expert[:, None] == slot_expert[None, :]
    copy_rank = jnp.sum(
        (same_expert & (slot_ids[None, :] < slot_ids[:, None])).astype(jnp.int32), axis=1
    )
    own_routes = lax.dynamic_slice_in_dim(route_expert, own_slot * tok_rows, tok_rows, 0).reshape(
        -1
    )
    holds = own_routes[:, None] == slot_expert[None, :]
    chosen = holds & (copy_rank[None, :] == 0)
    target = jnp.sum(jnp.where(chosen, slot_ids[None, :], 0), axis=1)
    onehot = chosen.astype(jnp.int32)
    position = jnp.sum(jnp.cumsum(onehot, axis=0) * onehot, axis=1) - 1
    buffer_index = target * capacity + position
    entry_rows = jnp.repeat(normed, TOPK, axis=0)
    outgoing = (
        jnp.zeros((slot_count * capacity, model_width), jnp.bfloat16)
        .at[buffer_index]
        .set(entry_rows)
    )
    outgoing = outgoing.reshape(slot_count, capacity, model_width)
    incoming = lax.all_to_all(outgoing, ("req", "exp"), split_axis=0, concat_axis=0, tiled=True)
    answered = expert_block(
        incoming.reshape(-1, model_width), expert_gate[0], expert_up[0], expert_down[0]
    ).reshape(slot_count, capacity, model_width)
    returned = lax.all_to_all(
        answered, ("req", "exp"), split_axis=0, concat_axis=0, tiled=True
    ).reshape(-1, model_width)
    expert_out = returned[buffer_index].reshape(tok_rows, TOPK, model_width)
    routed = jnp.sum(expert_out.astype(jnp.float32) * route_gate[:, :, None], axis=1)
    return (stream + shared_scale[:, None] * shared_out + routed).astype(jnp.bfloat16)


def solution(mesh):
    placed = (
        P(("req", "exp"), None),
        P(("req", "exp"), None),
        P(("req", "exp"), None, None),
        P(("req", "exp"), None, None),
        P("req", None),
        P("req"),
        P("req"),
        P("exp", None),
        P(),
        P(("req", "exp"), None, None),
        P(("req", "exp"), None, None),
        P(("req", "exp"), None, None),
        P(None, "exp"),
        P(None, "exp"),
        P("exp", None),
        P(),
        P(),
        P(),
        P(("req", "exp"), None),
    )
    return jax.shard_map(
        shards, mesh=mesh, in_specs=placed, out_specs=P(("req", "exp"), None), check_vma=False
    )
```

```python
import jax
import jax.numpy as jnp
from jax import lax
from jax.experimental import pallas as pl
from jax.sharding import PartitionSpec as P

HEADS = 16
HEAD_DIM = 128
TOPK = 4


def expert_block(rows, gate_w, up_w, down_w):
    gate = jnp.dot(rows, gate_w, preferred_element_type=jnp.float32)
    upper = jnp.dot(rows, up_w, preferred_element_type=jnp.float32)
    hidden = (jax.nn.silu(gate) * upper).astype(jnp.bfloat16)
    return jnp.dot(hidden, down_w, preferred_element_type=jnp.float32).astype(jnp.bfloat16)


def rms_normed(stream, norm_gain):
    scale_row = lax.rsqrt(jnp.mean(stream * stream, axis=1, keepdims=True) + 1e-06)
    return (stream * scale_row * norm_gain[None, :]).astype(jnp.bfloat16)


def head_attention_kernel(q_ref, k_ref, v_ref, rreq_ref, rpos_ref, kreq_ref, kpos_ref, o_ref):
    scores = lax.dot_general(
        q_ref[...], k_ref[...], (((1,), (1,)), ((), ())), preferred_element_type=jnp.float32
    ) * HEAD_DIM ** (-0.5)
    visible = (rreq_ref[...] == kreq_ref[...]) & (kpos_ref[...] <= rpos_ref[...])
    scores = jnp.where(visible, scores, -1e30)
    top = jnp.max(scores, axis=1, keepdims=True)
    weights = jnp.where(visible, jnp.exp(scores - top), 0.0)
    denominators = jnp.sum(weights, axis=1, keepdims=True)
    numerators = jnp.dot(
        weights.astype(jnp.bfloat16), v_ref[...], preferred_element_type=jnp.float32
    )
    o_ref[...] = (numerators / denominators).astype(o_ref.dtype)


def head_attention(query_cols, key_cols, value_cols, row_request, row_position, key_request, key_position):
    rows, width = query_cols.shape
    keys = key_cols.shape[0]
    tile = 128
    row_spec = pl.BlockSpec((tile, width), lambda i: (i, 0))
    whole = pl.BlockSpec((keys, width), lambda i: (0, 0))
    row_int = pl.BlockSpec((tile, 1), lambda i: (i, 0))
    key_int = pl.BlockSpec((1, keys), lambda i: (0, 0))
    return pl.pallas_call(
        head_attention_kernel,
        grid=(rows // tile,),
        out_shape=jax.ShapeDtypeStruct((rows, width), jnp.bfloat16),
        in_specs=[row_spec, whole, whole, row_int, row_int, key_int, key_int],
        out_specs=row_spec,
        cost_estimate=pl.CostEstimate(
            flops=4 * rows * keys * width, transcendentals=rows * keys, bytes_accessed=3 * keys * width * 2
        ),
    )(
        query_cols,
        key_cols,
        value_cols,
        row_request.reshape(rows, 1),
        row_position.reshape(rows, 1),
        key_request.reshape(1, keys),
        key_position.reshape(1, keys),
    )


def gather_exp(piece, count):
    spread = jnp.broadcast_to(piece[None], (count,) + piece.shape)
    got = lax.all_to_all(spread, "exp", 0, 0, tiled=True)
    return got.reshape((count * piece.shape[0],) + piece.shape[1:])


def shards(
    resid,
    queries,
    cache_key,
    cache_value,
    page_table,
    row_request,
    row_position,
    out_proj,
    norm_gain,
    expert_gate,
    expert_up,
    expert_down,
    shared_gate,
    shared_up,
    shared_down,
    shared_scalar,
    slot_expert,
    route_expert,
    route_gate,
):
    exp_count = lax.axis_size("exp")
    req_count = lax.axis_size("req")
    slot_count = exp_count * req_count
    exp_index = lax.axis_index("exp")
    own_slot = lax.axis_index("req") * exp_count + exp_index
    tok_rows = resid.shape[0]
    model_width = resid.shape[1]
    group_rows = row_request.shape[0]
    pages_here = cache_key.shape[0]
    page_len = cache_key.shape[1]
    req_slots = page_table.shape[0]
    max_pages = page_table.shape[1]
    capacity = 3 * tok_rows * TOPK // slot_count

    key_count = pages_here * page_len
    group_keys = exp_count * key_count
    by_head = jnp.concatenate(
        [
            queries.reshape(tok_rows, HEADS, HEAD_DIM).transpose(1, 0, 2),
            cache_key.reshape(key_count, HEADS, HEAD_DIM).transpose(1, 0, 2),
            cache_value.reshape(key_count, HEADS, HEAD_DIM).transpose(1, 0, 2),
        ],
        axis=1,
    )
    got_cols = lax.all_to_all(by_head, "exp", 0, 0, tiled=True)
    query_cols = got_cols[:, :tok_rows].reshape(group_rows, HEAD_DIM)
    key_cols = got_cols[:, tok_rows:tok_rows + key_count].reshape(group_keys, HEAD_DIM)
    value_cols = got_cols[:, tok_rows + key_count:].reshape(group_keys, HEAD_DIM)
    page_ids = jnp.arange(exp_count * pages_here, dtype=jnp.int32)
    hits = (page_table[None, :, :] == page_ids[:, None, None]).astype(jnp.int32)
    page_request = jnp.sum(
        hits * jnp.arange(req_slots, dtype=jnp.int32)[None, :, None], axis=(1, 2)
    )
    page_slot = jnp.sum(hits * jnp.arange(max_pages, dtype=jnp.int32)[None, None, :], axis=(1, 2))
    key_position = (
        page_slot[:, None] * page_len + jnp.arange(page_len, dtype=jnp.int32)[None, :]
    ).reshape(-1)
    key_request = jnp.repeat(page_request, page_len)
    attention = head_attention(
        query_cols, key_cols, value_cols, row_request, row_position, key_request, key_position
    )
    mixed_part = jnp.dot(attention, out_proj, preferred_element_type=jnp.float32)
    mixed = jnp.sum(
        lax.all_to_all(
            mixed_part.astype(jnp.bfloat16).reshape(exp_count, tok_rows, model_width),
            "exp", 0, 0, tiled=True,
        ).astype(jnp.float32),
        axis=0,
    )
    stream = resid.astype(jnp.float32) + mixed
    normed = rms_normed(stream, norm_gain)

    piece = lax.all_gather(normed, "exp", axis=0, tiled=True)
    gate = jnp.dot(piece, shared_gate, preferred_element_type=jnp.float32)
    upper = jnp.dot(piece, shared_up, preferred_element_type=jnp.float32)
    shared_hidden = (jax.nn.silu(gate) * upper).astype(jnp.bfloat16)
    shared_part = jnp.dot(
        shared_hidden, shared_down, preferred_element_type=jnp.float32
    ).astype(jnp.bfloat16)
    shared_out = lax.psum_scatter(
        shared_part, "exp", scatter_dimension=0, tiled=True
    ).astype(jnp.float32)
    shared_scale = jax.nn.sigmoid(
        jnp.dot(normed, shared_scalar, preferred_element_type=jnp.float32)
    )

    slot_ids = jnp.arange(slot_count, dtype=jnp.int32)
    same_expert = slot_expert[:, None] == slot_expert[None, :]
    copy_rank = jnp.sum(
        (same_expert & (slot_ids[None, :] < slot_ids[:, None])).astype(jnp.int32), axis=1
    )
    own_routes = lax.dynamic_slice_in_dim(route_expert, own_slot * tok_rows, tok_rows, 0).reshape(
        -1
    )
    holds = own_routes[:, None] == slot_expert[None, :]
    chosen = holds & (copy_rank[None, :] == 0)
    target = jnp.sum(jnp.where(chosen, slot_ids[None, :], 0), axis=1)
    onehot = chosen.astype(jnp.int32)
    position = jnp.sum(jnp.cumsum(onehot, axis=0) * onehot, axis=1) - 1
    places = jnp.arange(capacity, dtype=jnp.int32)
    entry_of = (target[:, None, None] == slot_ids[None, :, None]) & (
        position[:, None, None] == places[None, None, :]
    )
    row_of_entry = jnp.arange(tok_rows * TOPK, dtype=jnp.int32) // TOPK
    row_match = row_of_entry[:, None] == jnp.arange(tok_rows, dtype=jnp.int32)[None, :]
    picks = jnp.einsum(
        "esc,ei->sci",
        entry_of.astype(jnp.bfloat16),
        row_match.astype(jnp.bfloat16),
        preferred_element_type=jnp.float32,
    ).astype(jnp.bfloat16)
    outgoing = jnp.einsum(
        "sci,id->scd", picks, normed, preferred_element_type=jnp.float32
    ).astype(jnp.bfloat16)
    incoming = lax.all_to_all(outgoing, ("req", "exp"), split_axis=0, concat_axis=0, tiled=True)
    answered = expert_block(incoming, expert_gate[0], expert_up[0], expert_down[0])
    returned = lax.all_to_all(answered, ("req", "exp"), split_axis=0, concat_axis=0, tiled=True)
    combine = jnp.sum(
        jnp.where(
            entry_of.reshape(tok_rows, TOPK, slot_count, capacity),
            route_gate[:, :, None, None],
            0.0,
        ),
        axis=1,
    )
    routed = jnp.einsum(
        "rsc,scd->rd",
        combine,
        returned.astype(jnp.float32),
        precision=lax.Precision.HIGHEST,
        preferred_element_type=jnp.float32,
    )
    return (stream + shared_scale[:, None] * shared_out + routed).astype(jnp.bfloat16)


def solution(mesh):
    placed = (
        P(("req", "exp"), None),
        P(("req", "exp"), None),
        P(("req", "exp"), None, None),
        P(("req", "exp"), None, None),
        P("req", None),
        P("req"),
        P("req"),
        P("exp", None),
        P(),
        P(("req", "exp"), None, None),
        P(("req", "exp"), None, None),
        P(("req", "exp"), None, None),
        P(None, "exp"),
        P(None, "exp"),
        P("exp", None),
        P(),
        P(),
        P(),
        P(("req", "exp"), None),
    )
    return jax.shard_map(
        shards, mesh=mesh, in_specs=placed, out_specs=P(("req", "exp"), None), check_vma=False
    )
```

```python
import jax
import jax.numpy as jnp
from jax import lax
from jax.experimental import pallas as pl
from jax.sharding import PartitionSpec as P

HEADS = 16
HEAD_DIM = 128
TOPK = 4


def expert_block(rows, gate_w, up_w, down_w):
    gate = jnp.dot(rows, gate_w, preferred_element_type=jnp.float32)
    upper = jnp.dot(rows, up_w, preferred_element_type=jnp.float32)
    hidden = (jax.nn.silu(gate) * upper).astype(jnp.bfloat16)
    return jnp.dot(hidden, down_w, preferred_element_type=jnp.float32).astype(jnp.bfloat16)


def rms_normed(stream, norm_gain):
    scale_row = lax.rsqrt(jnp.mean(stream * stream, axis=1, keepdims=True) + 1e-06)
    return (stream * scale_row * norm_gain[None, :]).astype(jnp.bfloat16)


def head_attention_kernel(q_ref, k_ref, v_ref, rreq_ref, rpos_ref, kreq_ref, kpos_ref, o_ref):
    scores = lax.dot_general(
        q_ref[...], k_ref[...], (((1,), (1,)), ((), ())), preferred_element_type=jnp.float32
    ) * HEAD_DIM ** (-0.5)
    visible = (rreq_ref[...] == kreq_ref[...]) & (kpos_ref[...] <= rpos_ref[...])
    scores = jnp.where(visible, scores, -1e30)
    top = jnp.max(scores, axis=1, keepdims=True)
    weights = jnp.where(visible, jnp.exp(scores - top), 0.0)
    denominators = jnp.sum(weights, axis=1, keepdims=True)
    numerators = jnp.dot(
        weights.astype(jnp.bfloat16), v_ref[...], preferred_element_type=jnp.float32
    )
    o_ref[...] = (numerators / denominators).astype(o_ref.dtype)


def head_attention(query_cols, key_cols, value_cols, row_request, row_position, key_request, key_position):
    rows, width = query_cols.shape
    keys = key_cols.shape[0]
    tile = 128
    row_spec = pl.BlockSpec((tile, width), lambda i: (i, 0))
    whole = pl.BlockSpec((keys, width), lambda i: (0, 0))
    row_int = pl.BlockSpec((tile, 1), lambda i: (i, 0))
    key_int = pl.BlockSpec((1, keys), lambda i: (0, 0))
    return pl.pallas_call(
        head_attention_kernel,
        grid=(rows // tile,),
        out_shape=jax.ShapeDtypeStruct((rows, width), jnp.bfloat16),
        in_specs=[row_spec, whole, whole, row_int, row_int, key_int, key_int],
        out_specs=row_spec,
        cost_estimate=pl.CostEstimate(
            flops=4 * rows * keys * width, transcendentals=rows * keys, bytes_accessed=3 * keys * width * 2
        ),
    )(
        query_cols,
        key_cols,
        value_cols,
        row_request.reshape(rows, 1),
        row_position.reshape(rows, 1),
        key_request.reshape(1, keys),
        key_position.reshape(1, keys),
    )


def gather_exp(piece, count):
    spread = jnp.broadcast_to(piece[None], (count,) + piece.shape)
    got = lax.all_to_all(spread, "exp", 0, 0, tiled=True)
    return got.reshape((count * piece.shape[0],) + piece.shape[1:])


def shards(
    resid,
    queries,
    cache_key,
    cache_value,
    page_table,
    row_request,
    row_position,
    out_proj,
    norm_gain,
    expert_gate,
    expert_up,
    expert_down,
    shared_gate,
    shared_up,
    shared_down,
    shared_scalar,
    slot_expert,
    route_expert,
    route_gate,
):
    exp_count = lax.axis_size("exp")
    req_count = lax.axis_size("req")
    slot_count = exp_count * req_count
    exp_index = lax.axis_index("exp")
    own_slot = lax.axis_index("req") * exp_count + exp_index
    tok_rows = resid.shape[0]
    model_width = resid.shape[1]
    group_rows = row_request.shape[0]
    pages_here = cache_key.shape[0]
    page_len = cache_key.shape[1]
    req_slots = page_table.shape[0]
    max_pages = page_table.shape[1]
    capacity = 3 * tok_rows * TOPK // slot_count

    key_count = pages_here * page_len
    group_keys = exp_count * key_count
    by_head = jnp.concatenate(
        [
            queries.reshape(tok_rows, HEADS, HEAD_DIM).transpose(1, 0, 2),
            cache_key.reshape(key_count, HEADS, HEAD_DIM).transpose(1, 0, 2),
            cache_value.reshape(key_count, HEADS, HEAD_DIM).transpose(1, 0, 2),
        ],
        axis=1,
    )
    got_cols = lax.all_to_all(by_head, "exp", 0, 0, tiled=True)
    query_cols = got_cols[:, :tok_rows].reshape(group_rows, HEAD_DIM)
    key_cols = got_cols[:, tok_rows:tok_rows + key_count].reshape(group_keys, HEAD_DIM)
    value_cols = got_cols[:, tok_rows + key_count:].reshape(group_keys, HEAD_DIM)
    page_ids = jnp.arange(exp_count * pages_here, dtype=jnp.int32)
    hits = (page_table[None, :, :] == page_ids[:, None, None]).astype(jnp.int32)
    page_request = jnp.sum(
        hits * jnp.arange(req_slots, dtype=jnp.int32)[None, :, None], axis=(1, 2)
    )
    page_slot = jnp.sum(hits * jnp.arange(max_pages, dtype=jnp.int32)[None, None, :], axis=(1, 2))
    key_position = (
        page_slot[:, None] * page_len + jnp.arange(page_len, dtype=jnp.int32)[None, :]
    ).reshape(-1)
    key_request = jnp.repeat(page_request, page_len)
    attention = head_attention(
        query_cols, key_cols, value_cols, row_request, row_position, key_request, key_position
    )
    mixed_part = jnp.dot(attention, out_proj, preferred_element_type=jnp.float32)
    mixed = jnp.sum(
        lax.all_to_all(
            mixed_part.astype(jnp.bfloat16).reshape(exp_count, tok_rows, model_width),
            "exp", 0, 0, tiled=True,
        ).astype(jnp.float32),
        axis=0,
    )
    stream = resid.astype(jnp.float32) + mixed
    normed = rms_normed(stream, norm_gain)

    piece = gather_exp(normed, exp_count)
    gate = jnp.dot(piece, shared_gate, preferred_element_type=jnp.float32)
    upper = jnp.dot(piece, shared_up, preferred_element_type=jnp.float32)
    shared_hidden = (jax.nn.silu(gate) * upper).astype(jnp.bfloat16)
    shared_part = jnp.dot(
        shared_hidden, shared_down, preferred_element_type=jnp.float32
    ).astype(jnp.bfloat16)
    shared_out = lax.psum_scatter(
        shared_part, "exp", scatter_dimension=0, tiled=True
    ).astype(jnp.float32)
    shared_scale = jax.nn.sigmoid(
        jnp.dot(normed, shared_scalar, preferred_element_type=jnp.float32)
    )

    slot_ids = jnp.arange(slot_count, dtype=jnp.int32)
    same_expert = slot_expert[:, None] == slot_expert[None, :]
    copy_rank = jnp.sum(
        (same_expert & (slot_ids[None, :] < slot_ids[:, None])).astype(jnp.int32), axis=1
    )
    own_routes = lax.dynamic_slice_in_dim(route_expert, own_slot * tok_rows, tok_rows, 0).reshape(
        -1
    )
    holds = own_routes[:, None] == slot_expert[None, :]
    chosen = holds & (copy_rank[None, :] == 0)
    target = jnp.sum(jnp.where(chosen, slot_ids[None, :], 0), axis=1)
    onehot = chosen.astype(jnp.int32)
    position = jnp.sum(jnp.cumsum(onehot, axis=0) * onehot, axis=1) - 1
    places = jnp.arange(capacity, dtype=jnp.int32)
    entry_of = (target[:, None, None] == slot_ids[None, :, None]) & (
        position[:, None, None] == places[None, None, :]
    )
    row_of_entry = jnp.arange(tok_rows * TOPK, dtype=jnp.int32) // TOPK
    row_match = row_of_entry[:, None] == jnp.arange(tok_rows, dtype=jnp.int32)[None, :]
    picks = jnp.einsum(
        "esc,ei->sci",
        entry_of.astype(jnp.bfloat16),
        row_match.astype(jnp.bfloat16),
        preferred_element_type=jnp.float32,
    ).astype(jnp.bfloat16)
    outgoing = jnp.einsum(
        "sci,id->scd", picks, normed, preferred_element_type=jnp.float32
    ).astype(jnp.bfloat16)
    incoming = lax.all_to_all(outgoing, ("req", "exp"), split_axis=0, concat_axis=0, tiled=True)
    answered = expert_block(incoming, expert_gate[0], expert_up[0], expert_down[0])
    returned = lax.all_to_all(answered, ("req", "exp"), split_axis=0, concat_axis=0, tiled=True)
    chosen_rows = jnp.einsum(
        "rksc,scd->rkd",
        entry_of.reshape(tok_rows, TOPK, slot_count, capacity).astype(jnp.bfloat16),
        returned,
        preferred_element_type=jnp.float32,
    )
    routed = jnp.sum(chosen_rows * route_gate[:, :, None], axis=1)
    return (stream + shared_scale[:, None] * shared_out + routed).astype(jnp.bfloat16)


def solution(mesh):
    placed = (
        P(("req", "exp"), None),
        P(("req", "exp"), None),
        P(("req", "exp"), None, None),
        P(("req", "exp"), None, None),
        P("req", None),
        P("req"),
        P("req"),
        P("exp", None),
        P(),
        P(("req", "exp"), None, None),
        P(("req", "exp"), None, None),
        P(("req", "exp"), None, None),
        P(None, "exp"),
        P(None, "exp"),
        P("exp", None),
        P(),
        P(),
        P(),
        P(("req", "exp"), None),
    )
    return jax.shard_map(
        shards, mesh=mesh, in_specs=placed, out_specs=P(("req", "exp"), None), check_vma=False
    )
```

```python
import jax
import jax.numpy as jnp
from jax import lax
from jax.experimental import pallas as pl
from jax.experimental.pallas import tpu as pltpu
from jax.sharding import PartitionSpec as P

HEADS = 16
HEAD_DIM = 128
TOPK = 4


def expert_block(rows, gate_w, up_w, down_w):
    gate = jnp.dot(rows, gate_w, preferred_element_type=jnp.float32)
    upper = jnp.dot(rows, up_w, preferred_element_type=jnp.float32)
    hidden = (jax.nn.silu(gate) * upper).astype(jnp.bfloat16)
    return jnp.dot(hidden, down_w, preferred_element_type=jnp.float32).astype(jnp.bfloat16)


def rms_normed(stream, norm_gain):
    scale_row = lax.rsqrt(jnp.mean(stream * stream, axis=1, keepdims=True) + 1e-06)
    return (stream * scale_row * norm_gain[None, :]).astype(jnp.bfloat16)


def head_attention_kernel(lo_ref, hi_ref, q_ref, k_ref, v_ref, first_ref, last_ref, o_ref):
    tile = pl.program_id(0)
    block = 128
    query = q_ref[...]
    first = first_ref[...]
    last = last_ref[...]

    def scores_of(b):
        start = pl.multiple_of(b * block, block)
        keys = k_ref[pl.ds(start, block), :]
        scores = lax.dot_general(
            query, keys, (((1,), (1,)), ((), ())), preferred_element_type=jnp.float32
        ) * HEAD_DIM ** (-0.5)
        index = start + lax.broadcasted_iota(jnp.int32, (1, block), 1)
        visible = (index >= first) & (index <= last)
        return jnp.where(visible, scores, -1e30), visible

    def top_step(b, top):
        return jnp.maximum(top, jnp.max(scores_of(b)[0], axis=1, keepdims=True))

    rows = query.shape[0]
    top = lax.fori_loop(
        lo_ref[tile], hi_ref[tile] + 1, top_step, jnp.full((rows, 1), -1e30, jnp.float32)
    )

    def sum_step(b, carry):
        den, num = carry
        scores, visible = scores_of(b)
        weights = jnp.where(visible, jnp.exp(scores - top), 0.0)
        start = pl.multiple_of(b * block, block)
        num = num + jnp.dot(
            weights.astype(jnp.bfloat16), v_ref[pl.ds(start, block), :],
            preferred_element_type=jnp.float32,
        )
        return den + jnp.sum(weights, axis=1, keepdims=True), num

    den, num = lax.fori_loop(
        lo_ref[tile],
        hi_ref[tile] + 1,
        sum_step,
        (jnp.zeros((rows, 1), jnp.float32), jnp.zeros((rows, HEAD_DIM), jnp.float32)),
    )
    o_ref[...] = (num / den).astype(o_ref.dtype)


def head_attention(query_cols, key_cols, value_cols, first_key, last_key):
    rows, width = query_cols.shape
    keys = key_cols.shape[0]
    tile = 128
    lo = jnp.min(first_key.reshape(rows // tile, tile), axis=1) // 128
    hi = jnp.max(last_key.reshape(rows // tile, tile), axis=1) // 128
    row_spec = pl.BlockSpec((tile, width), lambda i, lo_ref, hi_ref: (i, 0))
    whole = pl.BlockSpec((keys, width), lambda i, lo_ref, hi_ref: (0, 0))
    row_int = pl.BlockSpec((tile, 1), lambda i, lo_ref, hi_ref: (i, 0))
    return pl.pallas_call(
        head_attention_kernel,
        grid_spec=pltpu.PrefetchScalarGridSpec(
            num_scalar_prefetch=2,
            grid=(rows // tile,),
            in_specs=[row_spec, whole, whole, row_int, row_int],
            out_specs=row_spec,
        ),
        out_shape=jax.ShapeDtypeStruct((rows, width), jnp.bfloat16),
        cost_estimate=pl.CostEstimate(
            flops=rows * keys * width, transcendentals=rows * keys // 4, bytes_accessed=3 * keys * width * 2
        ),
    )(
        lo.astype(jnp.int32),
        hi.astype(jnp.int32),
        query_cols,
        key_cols,
        value_cols,
        first_key.reshape(rows, 1),
        last_key.reshape(rows, 1),
    )


def gather_exp(piece, count):
    spread = jnp.broadcast_to(piece[None], (count,) + piece.shape)
    got = lax.all_to_all(spread, "exp", 0, 0, tiled=True)
    return got.reshape((count * piece.shape[0],) + piece.shape[1:])


def shards(
    resid,
    queries,
    cache_key,
    cache_value,
    page_table,
    row_request,
    row_position,
    out_proj,
    norm_gain,
    expert_gate,
    expert_up,
    expert_down,
    shared_gate,
    shared_up,
    shared_down,
    shared_scalar,
    slot_expert,
    route_expert,
    route_gate,
):
    exp_count = lax.axis_size("exp")
    req_count = lax.axis_size("req")
    slot_count = exp_count * req_count
    exp_index = lax.axis_index("exp")
    own_slot = lax.axis_index("req") * exp_count + exp_index
    tok_rows = resid.shape[0]
    model_width = resid.shape[1]
    group_rows = row_request.shape[0]
    pages_here = cache_key.shape[0]
    page_len = cache_key.shape[1]
    req_slots = page_table.shape[0]
    max_pages = page_table.shape[1]
    capacity = 3 * tok_rows * TOPK // slot_count

    key_count = pages_here * page_len
    group_keys = exp_count * key_count
    by_head = jnp.concatenate(
        [
            queries.reshape(tok_rows, HEADS, HEAD_DIM).transpose(1, 0, 2),
            cache_key.reshape(key_count, HEADS, HEAD_DIM).transpose(1, 0, 2),
            cache_value.reshape(key_count, HEADS, HEAD_DIM).transpose(1, 0, 2),
        ],
        axis=1,
    )
    got_cols = lax.all_to_all(by_head, "exp", 0, 0, tiled=True)
    query_cols = got_cols[:, :tok_rows].reshape(group_rows, HEAD_DIM)
    key_cols = got_cols[:, tok_rows:tok_rows + key_count].reshape(group_keys, HEAD_DIM)
    value_cols = got_cols[:, tok_rows + key_count:].reshape(group_keys, HEAD_DIM)
    group_pages = exp_count * pages_here
    page_order = page_table.reshape(-1)
    pick_page = (
        page_order[:, None] == jnp.arange(group_pages, dtype=jnp.int32)[None, :]
    ).astype(jnp.bfloat16)
    sorted_keys = jnp.dot(
        pick_page, key_cols.reshape(group_pages, page_len * HEAD_DIM),
        preferred_element_type=jnp.float32,
    ).astype(jnp.bfloat16).reshape(group_keys, HEAD_DIM)
    sorted_values = jnp.dot(
        pick_page, value_cols.reshape(group_pages, page_len * HEAD_DIM),
        preferred_element_type=jnp.float32,
    ).astype(jnp.bfloat16).reshape(group_keys, HEAD_DIM)
    first_key = row_request * (max_pages * page_len)
    attention = head_attention(
        query_cols, sorted_keys, sorted_values, first_key, first_key + row_position
    )
    mixed_part = jnp.dot(attention, out_proj, preferred_element_type=jnp.float32)
    mixed = jnp.sum(
        lax.all_to_all(
            mixed_part.astype(jnp.bfloat16).reshape(exp_count, tok_rows, model_width),
            "exp", 0, 0, tiled=True,
        ).astype(jnp.float32),
        axis=0,
    )
    stream = resid.astype(jnp.float32) + mixed
    normed = rms_normed(stream, norm_gain)

    piece = lax.all_gather(normed, "exp", axis=0, tiled=True)
    gate = jnp.dot(piece, shared_gate, preferred_element_type=jnp.float32)
    upper = jnp.dot(piece, shared_up, preferred_element_type=jnp.float32)
    shared_hidden = (jax.nn.silu(gate) * upper).astype(jnp.bfloat16)
    shared_part = jnp.dot(
        shared_hidden, shared_down, preferred_element_type=jnp.float32
    ).astype(jnp.bfloat16)
    shared_out = lax.psum_scatter(
        shared_part, "exp", scatter_dimension=0, tiled=True
    ).astype(jnp.float32)
    shared_scale = jax.nn.sigmoid(
        jnp.dot(normed, shared_scalar, preferred_element_type=jnp.float32)
    )

    slot_ids = jnp.arange(slot_count, dtype=jnp.int32)
    same_expert = slot_expert[:, None] == slot_expert[None, :]
    copy_rank = jnp.sum(
        (same_expert & (slot_ids[None, :] < slot_ids[:, None])).astype(jnp.int32), axis=1
    )
    own_routes = lax.dynamic_slice_in_dim(route_expert, own_slot * tok_rows, tok_rows, 0).reshape(
        -1
    )
    holds = own_routes[:, None] == slot_expert[None, :]
    chosen = holds & (copy_rank[None, :] == 0)
    target = jnp.sum(jnp.where(chosen, slot_ids[None, :], 0), axis=1)
    onehot = chosen.astype(jnp.int32)
    position = jnp.sum(jnp.cumsum(onehot, axis=0) * onehot, axis=1) - 1
    buffer_index = target * capacity + position
    entry_rows = jnp.repeat(normed, TOPK, axis=0)
    outgoing = (
        jnp.zeros((slot_count * capacity, model_width), jnp.bfloat16)
        .at[buffer_index]
        .set(entry_rows)
    )
    outgoing = outgoing.reshape(slot_count, capacity, model_width)
    incoming = lax.all_to_all(outgoing, ("req", "exp"), split_axis=0, concat_axis=0, tiled=True)
    answered = expert_block(
        incoming.reshape(-1, model_width), expert_gate[0], expert_up[0], expert_down[0]
    ).reshape(slot_count, capacity, model_width)
    returned = lax.all_to_all(
        answered, ("req", "exp"), split_axis=0, concat_axis=0, tiled=True
    ).reshape(-1, model_width)
    expert_out = returned[buffer_index].reshape(tok_rows, TOPK, model_width)
    routed = jnp.sum(expert_out.astype(jnp.float32) * route_gate[:, :, None], axis=1)
    return (stream + shared_scale[:, None] * shared_out + routed).astype(jnp.bfloat16)


def solution(mesh):
    placed = (
        P(("req", "exp"), None),
        P(("req", "exp"), None),
        P(("req", "exp"), None, None),
        P(("req", "exp"), None, None),
        P("req", None),
        P("req"),
        P("req"),
        P("exp", None),
        P(),
        P(("req", "exp"), None, None),
        P(("req", "exp"), None, None),
        P(("req", "exp"), None, None),
        P(None, "exp"),
        P(None, "exp"),
        P("exp", None),
        P(),
        P(),
        P(),
        P(("req", "exp"), None),
    )
    return jax.shard_map(
        shards, mesh=mesh, in_specs=placed, out_specs=P(("req", "exp"), None), check_vma=False
    )
```

```python
import jax
import jax.numpy as jnp
from jax import lax
from jax.experimental import pallas as pl
from jax.sharding import PartitionSpec as P

HEADS = 16
HEAD_DIM = 128
TOPK = 4


def expert_block(rows, gate_w, up_w, down_w):
    gate = jnp.dot(rows, gate_w, preferred_element_type=jnp.float32)
    upper = jnp.dot(rows, up_w, preferred_element_type=jnp.float32)
    hidden = (jax.nn.silu(gate) * upper).astype(jnp.bfloat16)
    return jnp.dot(hidden, down_w, preferred_element_type=jnp.float32).astype(jnp.bfloat16)


def rms_normed(stream, norm_gain):
    scale_row = lax.rsqrt(jnp.mean(stream * stream, axis=1, keepdims=True) + 1e-06)
    return (stream * scale_row * norm_gain[None, :]).astype(jnp.bfloat16)


def head_attention_kernel(q_ref, k_ref, v_ref, rreq_ref, rpos_ref, kreq_ref, kpos_ref, o_ref):
    scores = lax.dot_general(
        q_ref[...], k_ref[...], (((1,), (1,)), ((), ())), preferred_element_type=jnp.float32
    ) * HEAD_DIM ** (-0.5)
    visible = (rreq_ref[...] == kreq_ref[...]) & (kpos_ref[...] <= rpos_ref[...])
    scores = jnp.where(visible, scores, -1e30)
    top = jnp.max(scores, axis=1, keepdims=True)
    weights = jnp.where(visible, jnp.exp(scores - top), 0.0)
    denominators = jnp.sum(weights, axis=1, keepdims=True)
    numerators = jnp.dot(
        weights.astype(jnp.bfloat16), v_ref[...], preferred_element_type=jnp.float32
    )
    o_ref[...] = (numerators / denominators).astype(o_ref.dtype)


def head_attention(query_cols, key_cols, value_cols, row_request, row_position, key_request, key_position):
    rows, width = query_cols.shape
    keys = key_cols.shape[0]
    tile = 128
    row_spec = pl.BlockSpec((tile, width), lambda i: (i, 0))
    whole = pl.BlockSpec((keys, width), lambda i: (0, 0))
    row_int = pl.BlockSpec((tile, 1), lambda i: (i, 0))
    key_int = pl.BlockSpec((1, keys), lambda i: (0, 0))
    return pl.pallas_call(
        head_attention_kernel,
        grid=(rows // tile,),
        out_shape=jax.ShapeDtypeStruct((rows, width), jnp.bfloat16),
        in_specs=[row_spec, whole, whole, row_int, row_int, key_int, key_int],
        out_specs=row_spec,
        cost_estimate=pl.CostEstimate(
            flops=4 * rows * keys * width, transcendentals=rows * keys, bytes_accessed=3 * keys * width * 2
        ),
    )(
        query_cols,
        key_cols,
        value_cols,
        row_request.reshape(rows, 1),
        row_position.reshape(rows, 1),
        key_request.reshape(1, keys),
        key_position.reshape(1, keys),
    )


def gather_exp(piece, count):
    spread = jnp.broadcast_to(piece[None], (count,) + piece.shape)
    got = lax.all_to_all(spread, "exp", 0, 0, tiled=True)
    return got.reshape((count * piece.shape[0],) + piece.shape[1:])


def shards(
    resid,
    queries,
    cache_key,
    cache_value,
    page_table,
    row_request,
    row_position,
    out_proj,
    norm_gain,
    expert_gate,
    expert_up,
    expert_down,
    shared_gate,
    shared_up,
    shared_down,
    shared_scalar,
    slot_expert,
    route_expert,
    route_gate,
):
    exp_count = lax.axis_size("exp")
    req_count = lax.axis_size("req")
    slot_count = exp_count * req_count
    exp_index = lax.axis_index("exp")
    own_slot = lax.axis_index("req") * exp_count + exp_index
    tok_rows = resid.shape[0]
    model_width = resid.shape[1]
    group_rows = row_request.shape[0]
    pages_here = cache_key.shape[0]
    page_len = cache_key.shape[1]
    req_slots = page_table.shape[0]
    max_pages = page_table.shape[1]
    capacity = 3 * tok_rows * TOPK // slot_count

    whole_proj = lax.all_gather(out_proj, "exp", axis=0, tiled=True)
    key_count = pages_here * page_len
    group_keys = exp_count * key_count
    by_head = jnp.concatenate(
        [
            queries.reshape(tok_rows, HEADS, HEAD_DIM).transpose(1, 0, 2),
            cache_key.reshape(key_count, HEADS, HEAD_DIM).transpose(1, 0, 2),
            cache_value.reshape(key_count, HEADS, HEAD_DIM).transpose(1, 0, 2),
        ],
        axis=1,
    )
    got_cols = lax.all_to_all(by_head, "exp", 0, 0, tiled=True)
    query_cols = got_cols[:, :tok_rows].reshape(group_rows, HEAD_DIM)
    key_cols = got_cols[:, tok_rows:tok_rows + key_count].reshape(group_keys, HEAD_DIM)
    value_cols = got_cols[:, tok_rows + key_count:].reshape(group_keys, HEAD_DIM)
    page_ids = jnp.arange(exp_count * pages_here, dtype=jnp.int32)
    hits = (page_table[None, :, :] == page_ids[:, None, None]).astype(jnp.int32)
    page_request = jnp.sum(
        hits * jnp.arange(req_slots, dtype=jnp.int32)[None, :, None], axis=(1, 2)
    )
    page_slot = jnp.sum(hits * jnp.arange(max_pages, dtype=jnp.int32)[None, None, :], axis=(1, 2))
    key_position = (
        page_slot[:, None] * page_len + jnp.arange(page_len, dtype=jnp.int32)[None, :]
    ).reshape(-1)
    key_request = jnp.repeat(page_request, page_len)
    attention = head_attention(
        query_cols, key_cols, value_cols, row_request, row_position, key_request, key_position
    )
    attention_rows = lax.all_to_all(
        attention.reshape(exp_count, tok_rows, HEAD_DIM), "exp", 0, 0, tiled=True
    )
    attention_rows = attention_rows.transpose(1, 0, 2).reshape(tok_rows, model_width)
    mixed = jnp.dot(attention_rows, whole_proj, preferred_element_type=jnp.float32)
    stream = resid.astype(jnp.float32) + mixed
    normed = rms_normed(stream, norm_gain)

    piece = lax.all_gather(normed, "exp", axis=0, tiled=True)
    gate = jnp.dot(piece, shared_gate, preferred_element_type=jnp.float32)
    upper = jnp.dot(piece, shared_up, preferred_element_type=jnp.float32)
    shared_hidden = (jax.nn.silu(gate) * upper).astype(jnp.bfloat16)
    shared_part = jnp.dot(
        shared_hidden, shared_down, preferred_element_type=jnp.float32
    ).astype(jnp.bfloat16)
    shared_out = lax.psum_scatter(
        shared_part, "exp", scatter_dimension=0, tiled=True
    ).astype(jnp.float32)
    shared_scale = jax.nn.sigmoid(
        jnp.dot(normed, shared_scalar, preferred_element_type=jnp.float32)
    )

    slot_ids = jnp.arange(slot_count, dtype=jnp.int32)
    same_expert = slot_expert[:, None] == slot_expert[None, :]
    copy_rank = jnp.sum(
        (same_expert & (slot_ids[None, :] < slot_ids[:, None])).astype(jnp.int32), axis=1
    )
    own_routes = lax.dynamic_slice_in_dim(route_expert, own_slot * tok_rows, tok_rows, 0).reshape(
        -1
    )
    holds = own_routes[:, None] == slot_expert[None, :]
    chosen = holds & (copy_rank[None, :] == 0)
    target = jnp.sum(jnp.where(chosen, slot_ids[None, :], 0), axis=1)
    onehot = chosen.astype(jnp.int32)
    position = jnp.sum(jnp.cumsum(onehot, axis=0) * onehot, axis=1) - 1
    buffer_index = target * capacity + position
    entry_rows = jnp.repeat(normed, TOPK, axis=0)
    outgoing = (
        jnp.zeros((slot_count * capacity, model_width), jnp.bfloat16)
        .at[buffer_index]
        .set(entry_rows)
    )
    outgoing = outgoing.reshape(slot_count, capacity, model_width)
    incoming = lax.all_to_all(outgoing, ("req", "exp"), split_axis=0, concat_axis=0, tiled=True)
    answered = expert_block(
        incoming.reshape(-1, model_width), expert_gate[0], expert_up[0], expert_down[0]
    ).reshape(slot_count, capacity, model_width)
    returned = lax.all_to_all(
        answered, ("req", "exp"), split_axis=0, concat_axis=0, tiled=True
    ).reshape(-1, model_width)
    expert_out = returned[buffer_index].reshape(tok_rows, TOPK, model_width)
    routed = jnp.sum(expert_out.astype(jnp.float32) * route_gate[:, :, None], axis=1)
    return (stream + shared_scale[:, None] * shared_out + routed).astype(jnp.bfloat16)


def solution(mesh):
    placed = (
        P(("req", "exp"), None),
        P(("req", "exp"), None),
        P(("req", "exp"), None, None),
        P(("req", "exp"), None, None),
        P("req", None),
        P("req"),
        P("req"),
        P("exp", None),
        P(),
        P(("req", "exp"), None, None),
        P(("req", "exp"), None, None),
        P(("req", "exp"), None, None),
        P(None, "exp"),
        P(None, "exp"),
        P("exp", None),
        P(),
        P(),
        P(),
        P(("req", "exp"), None),
    )
    return jax.shard_map(
        shards, mesh=mesh, in_specs=placed, out_specs=P(("req", "exp"), None), check_vma=False
    )
```

```python
import jax
import jax.numpy as jnp
from jax import lax
from jax.experimental import pallas as pl
from jax.sharding import PartitionSpec as P

HEADS = 16
HEAD_DIM = 128
TOPK = 4


def expert_block(rows, gate_w, up_w, down_w):
    gate = jnp.dot(rows, gate_w, preferred_element_type=jnp.float32)
    upper = jnp.dot(rows, up_w, preferred_element_type=jnp.float32)
    hidden = (jax.nn.silu(gate) * upper).astype(jnp.bfloat16)
    return jnp.dot(hidden, down_w, preferred_element_type=jnp.float32).astype(jnp.bfloat16)


def rms_normed(stream, norm_gain):
    scale_row = lax.rsqrt(jnp.mean(stream * stream, axis=1, keepdims=True) + 1e-06)
    return (stream * scale_row * norm_gain[None, :]).astype(jnp.bfloat16)


def head_attention_kernel(q_ref, k_ref, v_ref, rreq_ref, rpos_ref, kreq_ref, kpos_ref, o_ref):
    scores = lax.dot_general(
        q_ref[...], k_ref[...], (((1,), (1,)), ((), ())), preferred_element_type=jnp.float32
    ) * HEAD_DIM ** (-0.5)
    visible = (rreq_ref[...] == kreq_ref[...]) & (kpos_ref[...] <= rpos_ref[...])
    scores = jnp.where(visible, scores, -1e30)
    top = jnp.max(scores, axis=1, keepdims=True)
    weights = jnp.where(visible, jnp.exp(scores - top), 0.0)
    denominators = jnp.sum(weights, axis=1, keepdims=True)
    numerators = jnp.dot(
        weights.astype(jnp.bfloat16), v_ref[...], preferred_element_type=jnp.float32
    )
    o_ref[...] = (numerators / denominators).astype(o_ref.dtype)


def head_attention(query_cols, key_cols, value_cols, row_request, row_position, key_request, key_position):
    rows, width = query_cols.shape
    keys = key_cols.shape[0]
    tile = 128
    row_spec = pl.BlockSpec((tile, width), lambda i: (i, 0))
    whole = pl.BlockSpec((keys, width), lambda i: (0, 0))
    row_int = pl.BlockSpec((tile, 1), lambda i: (i, 0))
    key_int = pl.BlockSpec((1, keys), lambda i: (0, 0))
    return pl.pallas_call(
        head_attention_kernel,
        grid=(rows // tile,),
        out_shape=jax.ShapeDtypeStruct((rows, width), jnp.bfloat16),
        in_specs=[row_spec, whole, whole, row_int, row_int, key_int, key_int],
        out_specs=row_spec,
        cost_estimate=pl.CostEstimate(
            flops=4 * rows * keys * width, transcendentals=rows * keys, bytes_accessed=3 * keys * width * 2
        ),
    )(
        query_cols,
        key_cols,
        value_cols,
        row_request.reshape(rows, 1),
        row_position.reshape(rows, 1),
        key_request.reshape(1, keys),
        key_position.reshape(1, keys),
    )


def gather_exp(piece, count):
    spread = jnp.broadcast_to(piece[None], (count,) + piece.shape)
    got = lax.all_to_all(spread, "exp", 0, 0, tiled=True)
    return got.reshape((count * piece.shape[0],) + piece.shape[1:])


def shards(
    resid,
    queries,
    cache_key,
    cache_value,
    page_table,
    row_request,
    row_position,
    out_proj,
    norm_gain,
    expert_gate,
    expert_up,
    expert_down,
    shared_gate,
    shared_up,
    shared_down,
    shared_scalar,
    slot_expert,
    route_expert,
    route_gate,
):
    exp_count = lax.axis_size("exp")
    req_count = lax.axis_size("req")
    slot_count = exp_count * req_count
    exp_index = lax.axis_index("exp")
    own_slot = lax.axis_index("req") * exp_count + exp_index
    tok_rows = resid.shape[0]
    model_width = resid.shape[1]
    group_rows = row_request.shape[0]
    pages_here = cache_key.shape[0]
    page_len = cache_key.shape[1]
    req_slots = page_table.shape[0]
    max_pages = page_table.shape[1]
    capacity = 3 * tok_rows * TOPK // slot_count

    whole_proj = lax.all_gather(out_proj, "exp", axis=0, tiled=True)
    key_count = pages_here * page_len
    group_keys = exp_count * key_count
    by_head = jnp.concatenate(
        [
            queries.reshape(tok_rows, HEADS, HEAD_DIM).transpose(1, 0, 2),
            cache_key.reshape(key_count, HEADS, HEAD_DIM).transpose(1, 0, 2),
            cache_value.reshape(key_count, HEADS, HEAD_DIM).transpose(1, 0, 2),
        ],
        axis=1,
    )
    got_cols = lax.all_to_all(by_head, "exp", 0, 0, tiled=True)
    query_cols = got_cols[:, :tok_rows].reshape(group_rows, HEAD_DIM)
    key_cols = got_cols[:, tok_rows:tok_rows + key_count].reshape(group_keys, HEAD_DIM)
    value_cols = got_cols[:, tok_rows + key_count:].reshape(group_keys, HEAD_DIM)
    page_ids = jnp.arange(exp_count * pages_here, dtype=jnp.int32)
    hits = (page_table[None, :, :] == page_ids[:, None, None]).astype(jnp.int32)
    page_request = jnp.sum(
        hits * jnp.arange(req_slots, dtype=jnp.int32)[None, :, None], axis=(1, 2)
    )
    page_slot = jnp.sum(hits * jnp.arange(max_pages, dtype=jnp.int32)[None, None, :], axis=(1, 2))
    key_position = (
        page_slot[:, None] * page_len + jnp.arange(page_len, dtype=jnp.int32)[None, :]
    ).reshape(-1)
    key_request = jnp.repeat(page_request, page_len)
    attention = head_attention(
        query_cols, key_cols, value_cols, row_request, row_position, key_request, key_position
    )
    attention_rows = lax.all_to_all(
        attention.reshape(exp_count, tok_rows, HEAD_DIM), "exp", 0, 0, tiled=True
    )
    attention_rows = attention_rows.transpose(1, 0, 2).reshape(tok_rows, model_width)
    mixed = jnp.dot(attention_rows, whole_proj, preferred_element_type=jnp.float32)
    stream = resid.astype(jnp.float32) + mixed
    normed = rms_normed(stream, norm_gain)

    piece = lax.all_gather(normed, "exp", axis=0, tiled=True)
    gate = jnp.dot(piece, shared_gate, preferred_element_type=jnp.float32)
    upper = jnp.dot(piece, shared_up, preferred_element_type=jnp.float32)
    shared_hidden = (jax.nn.silu(gate) * upper).astype(jnp.bfloat16)
    shared_part = jnp.dot(
        shared_hidden, shared_down, preferred_element_type=jnp.float32
    ).astype(jnp.bfloat16)
    shared_out = lax.psum_scatter(
        shared_part, "exp", scatter_dimension=0, tiled=True
    ).astype(jnp.float32)
    shared_scale = jax.nn.sigmoid(
        jnp.dot(normed, shared_scalar, preferred_element_type=jnp.float32)
    )

    slot_ids = jnp.arange(slot_count, dtype=jnp.int32)
    same_expert = slot_expert[:, None] == slot_expert[None, :]
    copy_rank = jnp.sum(
        (same_expert & (slot_ids[None, :] < slot_ids[:, None])).astype(jnp.int32), axis=1
    )
    own_routes = lax.dynamic_slice_in_dim(route_expert, own_slot * tok_rows, tok_rows, 0).reshape(
        -1
    )
    holds = own_routes[:, None] == slot_expert[None, :]
    chosen = holds & (copy_rank[None, :] == 0)
    target = jnp.sum(jnp.where(chosen, slot_ids[None, :], 0), axis=1)
    onehot = chosen.astype(jnp.int32)
    position = jnp.sum(jnp.cumsum(onehot, axis=0) * onehot, axis=1) - 1
    places = jnp.arange(capacity, dtype=jnp.int32)
    entry_of = (target[:, None, None] == slot_ids[None, :, None]) & (
        position[:, None, None] == places[None, None, :]
    )
    row_of_entry = jnp.arange(tok_rows * TOPK, dtype=jnp.int32) // TOPK
    row_match = row_of_entry[:, None] == jnp.arange(tok_rows, dtype=jnp.int32)[None, :]
    picks = jnp.einsum(
        "esc,ei->sci",
        entry_of.astype(jnp.bfloat16),
        row_match.astype(jnp.bfloat16),
        preferred_element_type=jnp.float32,
    ).astype(jnp.bfloat16)
    outgoing = jnp.einsum(
        "sci,id->scd", picks, normed, preferred_element_type=jnp.float32
    ).astype(jnp.bfloat16)
    incoming = lax.all_to_all(outgoing, ("req", "exp"), split_axis=0, concat_axis=0, tiled=True)
    answered = expert_block(incoming, expert_gate[0], expert_up[0], expert_down[0])
    returned = lax.all_to_all(answered, ("req", "exp"), split_axis=0, concat_axis=0, tiled=True)
    chosen_rows = jnp.einsum(
        "rksc,scd->rkd",
        entry_of.reshape(tok_rows, TOPK, slot_count, capacity).astype(jnp.bfloat16),
        returned,
        preferred_element_type=jnp.float32,
    )
    routed = jnp.sum(chosen_rows * route_gate[:, :, None], axis=1)
    return (stream + shared_scale[:, None] * shared_out + routed).astype(jnp.bfloat16)


def solution(mesh):
    placed = (
        P(("req", "exp"), None),
        P(("req", "exp"), None),
        P(("req", "exp"), None, None),
        P(("req", "exp"), None, None),
        P("req", None),
        P("req"),
        P("req"),
        P("exp", None),
        P(),
        P(("req", "exp"), None, None),
        P(("req", "exp"), None, None),
        P(("req", "exp"), None, None),
        P(None, "exp"),
        P(None, "exp"),
        P("exp", None),
        P(),
        P(),
        P(),
        P(("req", "exp"), None),
    )
    return jax.shard_map(
        shards, mesh=mesh, in_specs=placed, out_specs=P(("req", "exp"), None), check_vma=False
    )
```

```python
import jax
import jax.numpy as jnp
from jax import lax
from jax.experimental import pallas as pl
from jax.sharding import PartitionSpec as P

HEADS = 16
HEAD_DIM = 128
TOPK = 4


def expert_block(rows, gate_w, up_w, down_w):
    gate = jnp.dot(rows, gate_w, preferred_element_type=jnp.float32)
    upper = jnp.dot(rows, up_w, preferred_element_type=jnp.float32)
    hidden = (jax.nn.silu(gate) * upper).astype(jnp.bfloat16)
    return jnp.dot(hidden, down_w, preferred_element_type=jnp.float32).astype(jnp.bfloat16)


def rms_normed(stream, norm_gain):
    scale_row = lax.rsqrt(jnp.mean(stream * stream, axis=1, keepdims=True) + 1e-06)
    return (stream * scale_row * norm_gain[None, :]).astype(jnp.bfloat16)


def head_attention_kernel(q_ref, k_ref, v_ref, rreq_ref, rpos_ref, kreq_ref, kpos_ref, o_ref):
    scores = lax.dot_general(
        q_ref[...], k_ref[...], (((1,), (1,)), ((), ())), preferred_element_type=jnp.float32
    ) * HEAD_DIM ** (-0.5)
    visible = (rreq_ref[...] == kreq_ref[...]) & (kpos_ref[...] <= rpos_ref[...])
    scores = jnp.where(visible, scores, -1e30)
    top = jnp.max(scores, axis=1, keepdims=True)
    weights = jnp.where(visible, jnp.exp(scores - top), 0.0)
    denominators = jnp.sum(weights, axis=1, keepdims=True)
    numerators = jnp.dot(
        weights.astype(jnp.bfloat16), v_ref[...], preferred_element_type=jnp.float32
    )
    o_ref[...] = (numerators / denominators).astype(o_ref.dtype)


def head_attention(query_cols, key_cols, value_cols, row_request, row_position, key_request, key_position):
    rows, width = query_cols.shape
    keys = key_cols.shape[0]
    tile = 128
    row_spec = pl.BlockSpec((tile, width), lambda i: (i, 0))
    whole = pl.BlockSpec((keys, width), lambda i: (0, 0))
    row_int = pl.BlockSpec((tile, 1), lambda i: (i, 0))
    key_int = pl.BlockSpec((1, keys), lambda i: (0, 0))
    return pl.pallas_call(
        head_attention_kernel,
        grid=(rows // tile,),
        out_shape=jax.ShapeDtypeStruct((rows, width), jnp.bfloat16),
        in_specs=[row_spec, whole, whole, row_int, row_int, key_int, key_int],
        out_specs=row_spec,
        cost_estimate=pl.CostEstimate(
            flops=4 * rows * keys * width, transcendentals=rows * keys, bytes_accessed=3 * keys * width * 2
        ),
    )(
        query_cols,
        key_cols,
        value_cols,
        row_request.reshape(rows, 1),
        row_position.reshape(rows, 1),
        key_request.reshape(1, keys),
        key_position.reshape(1, keys),
    )


def gather_exp(piece, count):
    spread = jnp.broadcast_to(piece[None], (count,) + piece.shape)
    got = lax.all_to_all(spread, "exp", 0, 0, tiled=True)
    return got.reshape((count * piece.shape[0],) + piece.shape[1:])


def shards(
    resid,
    queries,
    cache_key,
    cache_value,
    page_table,
    row_request,
    row_position,
    out_proj,
    norm_gain,
    expert_gate,
    expert_up,
    expert_down,
    shared_gate,
    shared_up,
    shared_down,
    shared_scalar,
    slot_expert,
    route_expert,
    route_gate,
):
    exp_count = lax.axis_size("exp")
    req_count = lax.axis_size("req")
    slot_count = exp_count * req_count
    exp_index = lax.axis_index("exp")
    own_slot = lax.axis_index("req") * exp_count + exp_index
    tok_rows = resid.shape[0]
    model_width = resid.shape[1]
    group_rows = row_request.shape[0]
    pages_here = cache_key.shape[0]
    page_len = cache_key.shape[1]
    req_slots = page_table.shape[0]
    max_pages = page_table.shape[1]
    capacity = 3 * tok_rows * TOPK // slot_count

    whole_proj = lax.all_gather(out_proj, "exp", axis=0, tiled=True)
    key_count = pages_here * page_len
    group_keys = exp_count * key_count
    by_head = jnp.concatenate(
        [
            queries.reshape(tok_rows, HEADS, HEAD_DIM).transpose(1, 0, 2),
            cache_key.reshape(key_count, HEADS, HEAD_DIM).transpose(1, 0, 2),
            cache_value.reshape(key_count, HEADS, HEAD_DIM).transpose(1, 0, 2),
        ],
        axis=1,
    )
    got_cols = lax.all_to_all(by_head, "exp", 0, 0, tiled=True)
    query_cols = got_cols[:, :tok_rows].reshape(group_rows, HEAD_DIM)
    key_cols = got_cols[:, tok_rows:tok_rows + key_count].reshape(group_keys, HEAD_DIM)
    value_cols = got_cols[:, tok_rows + key_count:].reshape(group_keys, HEAD_DIM)
    page_ids = jnp.arange(exp_count * pages_here, dtype=jnp.int32)
    hits = (page_table[None, :, :] == page_ids[:, None, None]).astype(jnp.int32)
    page_request = jnp.sum(
        hits * jnp.arange(req_slots, dtype=jnp.int32)[None, :, None], axis=(1, 2)
    )
    page_slot = jnp.sum(hits * jnp.arange(max_pages, dtype=jnp.int32)[None, None, :], axis=(1, 2))
    key_position = (
        page_slot[:, None] * page_len + jnp.arange(page_len, dtype=jnp.int32)[None, :]
    ).reshape(-1)
    key_request = jnp.repeat(page_request, page_len)
    attention = head_attention(
        query_cols, key_cols, value_cols, row_request, row_position, key_request, key_position
    )
    attention_rows = lax.all_to_all(
        attention.reshape(exp_count, tok_rows, HEAD_DIM), "exp", 0, 0, tiled=True
    )
    attention_rows = attention_rows.transpose(1, 0, 2).reshape(tok_rows, model_width)
    mixed = jnp.dot(attention_rows, whole_proj, preferred_element_type=jnp.float32)
    stream = resid.astype(jnp.float32) + mixed
    normed = rms_normed(stream, norm_gain)

    piece = lax.all_gather(normed, "exp", axis=0, tiled=True)
    gate = jnp.dot(piece, shared_gate, preferred_element_type=jnp.float32)
    upper = jnp.dot(piece, shared_up, preferred_element_type=jnp.float32)
    shared_hidden = (jax.nn.silu(gate) * upper).astype(jnp.bfloat16)
    shared_part = jnp.dot(
        shared_hidden, shared_down, preferred_element_type=jnp.float32
    ).astype(jnp.bfloat16)
    half = model_width // 2
    shared_left = jnp.sum(
        lax.all_to_all(
            shared_part[:, :half].reshape(exp_count, tok_rows, half), "exp", 0, 0, tiled=True
        ).astype(jnp.float32),
        axis=0,
    )
    shared_right = lax.psum_scatter(
        shared_part[:, half:], "exp", scatter_dimension=0, tiled=True
    ).astype(jnp.float32)
    shared_out = jnp.concatenate([shared_left, shared_right], axis=1)
    shared_scale = jax.nn.sigmoid(
        jnp.dot(normed, shared_scalar, preferred_element_type=jnp.float32)
    )

    slot_ids = jnp.arange(slot_count, dtype=jnp.int32)
    same_expert = slot_expert[:, None] == slot_expert[None, :]
    copy_rank = jnp.sum(
        (same_expert & (slot_ids[None, :] < slot_ids[:, None])).astype(jnp.int32), axis=1
    )
    own_routes = lax.dynamic_slice_in_dim(route_expert, own_slot * tok_rows, tok_rows, 0).reshape(
        -1
    )
    holds = own_routes[:, None] == slot_expert[None, :]
    chosen = holds & (copy_rank[None, :] == 0)
    target = jnp.sum(jnp.where(chosen, slot_ids[None, :], 0), axis=1)
    onehot = chosen.astype(jnp.int32)
    position = jnp.sum(jnp.cumsum(onehot, axis=0) * onehot, axis=1) - 1
    places = jnp.arange(capacity, dtype=jnp.int32)
    entry_of = (target[:, None, None] == slot_ids[None, :, None]) & (
        position[:, None, None] == places[None, None, :]
    )
    row_of_entry = jnp.arange(tok_rows * TOPK, dtype=jnp.int32) // TOPK
    row_match = row_of_entry[:, None] == jnp.arange(tok_rows, dtype=jnp.int32)[None, :]
    picks = jnp.einsum(
        "esc,ei->sci",
        entry_of.astype(jnp.bfloat16),
        row_match.astype(jnp.bfloat16),
        preferred_element_type=jnp.float32,
    ).astype(jnp.bfloat16)
    outgoing = jnp.einsum(
        "sci,id->scd", picks, normed, preferred_element_type=jnp.float32
    ).astype(jnp.bfloat16)
    incoming = lax.all_to_all(outgoing, ("req", "exp"), split_axis=0, concat_axis=0, tiled=True)
    answered = expert_block(incoming, expert_gate[0], expert_up[0], expert_down[0])
    returned = lax.all_to_all(answered, ("req", "exp"), split_axis=0, concat_axis=0, tiled=True)
    chosen_rows = jnp.einsum(
        "rksc,scd->rkd",
        entry_of.reshape(tok_rows, TOPK, slot_count, capacity).astype(jnp.bfloat16),
        returned,
        preferred_element_type=jnp.float32,
    )
    routed = jnp.sum(chosen_rows * route_gate[:, :, None], axis=1)
    return (stream + shared_scale[:, None] * shared_out + routed).astype(jnp.bfloat16)


def solution(mesh):
    placed = (
        P(("req", "exp"), None),
        P(("req", "exp"), None),
        P(("req", "exp"), None, None),
        P(("req", "exp"), None, None),
        P("req", None),
        P("req"),
        P("req"),
        P("exp", None),
        P(),
        P(("req", "exp"), None, None),
        P(("req", "exp"), None, None),
        P(("req", "exp"), None, None),
        P(None, "exp"),
        P(None, "exp"),
        P("exp", None),
        P(),
        P(),
        P(),
        P(("req", "exp"), None),
    )
    return jax.shard_map(
        shards, mesh=mesh, in_specs=placed, out_specs=P(("req", "exp"), None), check_vma=False
    )
```

```python
import jax
import jax.numpy as jnp
from jax import lax
from jax.experimental import pallas as pl
from jax.sharding import PartitionSpec as P

HEADS = 16
HEAD_DIM = 128
TOPK = 4


def expert_block(rows, gate_w, up_w, down_w):
    gate = jnp.dot(rows, gate_w, preferred_element_type=jnp.float32)
    upper = jnp.dot(rows, up_w, preferred_element_type=jnp.float32)
    hidden = (jax.nn.silu(gate) * upper).astype(jnp.bfloat16)
    return jnp.dot(hidden, down_w, preferred_element_type=jnp.float32).astype(jnp.bfloat16)


def rms_normed(stream, norm_gain):
    scale_row = lax.rsqrt(jnp.mean(stream * stream, axis=1, keepdims=True) + 1e-06)
    return (stream * scale_row * norm_gain[None, :]).astype(jnp.bfloat16)


def head_attention_kernel(q_ref, k_ref, v_ref, rreq_ref, rpos_ref, kreq_ref, kpos_ref, o_ref):
    scores = lax.dot_general(
        q_ref[...], k_ref[...], (((1,), (1,)), ((), ())), preferred_element_type=jnp.float32
    ) * HEAD_DIM ** (-0.5)
    visible = (rreq_ref[...] == kreq_ref[...]) & (kpos_ref[...] <= rpos_ref[...])
    scores = jnp.where(visible, scores, -1e30)
    top = jnp.max(scores, axis=1, keepdims=True)
    weights = jnp.where(visible, jnp.exp(scores - top), 0.0)
    denominators = jnp.sum(weights, axis=1, keepdims=True)
    numerators = jnp.dot(
        weights.astype(jnp.bfloat16), v_ref[...], preferred_element_type=jnp.float32
    )
    o_ref[...] = (numerators / denominators).astype(o_ref.dtype)


def head_attention(query_cols, key_cols, value_cols, row_request, row_position, key_request, key_position):
    rows, width = query_cols.shape
    keys = key_cols.shape[0]
    tile = 128
    row_spec = pl.BlockSpec((tile, width), lambda i: (i, 0))
    whole = pl.BlockSpec((keys, width), lambda i: (0, 0))
    row_int = pl.BlockSpec((tile, 1), lambda i: (i, 0))
    key_int = pl.BlockSpec((1, keys), lambda i: (0, 0))
    return pl.pallas_call(
        head_attention_kernel,
        grid=(rows // tile,),
        out_shape=jax.ShapeDtypeStruct((rows, width), jnp.bfloat16),
        in_specs=[row_spec, whole, whole, row_int, row_int, key_int, key_int],
        out_specs=row_spec,
        cost_estimate=pl.CostEstimate(
            flops=4 * rows * keys * width, transcendentals=rows * keys, bytes_accessed=3 * keys * width * 2
        ),
    )(
        query_cols,
        key_cols,
        value_cols,
        row_request.reshape(rows, 1),
        row_position.reshape(rows, 1),
        key_request.reshape(1, keys),
        key_position.reshape(1, keys),
    )


def gather_exp(piece, count):
    spread = jnp.broadcast_to(piece[None], (count,) + piece.shape)
    got = lax.all_to_all(spread, "exp", 0, 0, tiled=True)
    return got.reshape((count * piece.shape[0],) + piece.shape[1:])


def shards(
    resid,
    queries,
    cache_key,
    cache_value,
    page_table,
    row_request,
    row_position,
    out_proj,
    norm_gain,
    expert_gate,
    expert_up,
    expert_down,
    shared_gate,
    shared_up,
    shared_down,
    shared_scalar,
    slot_expert,
    route_expert,
    route_gate,
):
    exp_count = lax.axis_size("exp")
    req_count = lax.axis_size("req")
    slot_count = exp_count * req_count
    exp_index = lax.axis_index("exp")
    own_slot = lax.axis_index("req") * exp_count + exp_index
    tok_rows = resid.shape[0]
    model_width = resid.shape[1]
    group_rows = row_request.shape[0]
    pages_here = cache_key.shape[0]
    page_len = cache_key.shape[1]
    req_slots = page_table.shape[0]
    max_pages = page_table.shape[1]
    capacity = 3 * tok_rows * TOPK // slot_count

    whole_proj = lax.all_gather(out_proj, "exp", axis=0, tiled=True)
    key_count = pages_here * page_len
    group_keys = exp_count * key_count
    by_head = jnp.concatenate(
        [
            queries.reshape(tok_rows, HEADS, HEAD_DIM).transpose(1, 0, 2),
            cache_key.reshape(key_count, HEADS, HEAD_DIM).transpose(1, 0, 2),
            cache_value.reshape(key_count, HEADS, HEAD_DIM).transpose(1, 0, 2),
        ],
        axis=1,
    )
    got_cols = lax.all_to_all(by_head, "exp", 0, 0, tiled=True)
    query_cols = got_cols[:, :tok_rows].reshape(group_rows, HEAD_DIM)
    key_cols = got_cols[:, tok_rows:tok_rows + key_count].reshape(group_keys, HEAD_DIM)
    value_cols = got_cols[:, tok_rows + key_count:].reshape(group_keys, HEAD_DIM)
    page_ids = jnp.arange(exp_count * pages_here, dtype=jnp.int32)
    hits = (page_table[None, :, :] == page_ids[:, None, None]).astype(jnp.int32)
    page_request = jnp.sum(
        hits * jnp.arange(req_slots, dtype=jnp.int32)[None, :, None], axis=(1, 2)
    )
    page_slot = jnp.sum(hits * jnp.arange(max_pages, dtype=jnp.int32)[None, None, :], axis=(1, 2))
    key_position = (
        page_slot[:, None] * page_len + jnp.arange(page_len, dtype=jnp.int32)[None, :]
    ).reshape(-1)
    key_request = jnp.repeat(page_request, page_len)
    attention = head_attention(
        query_cols, key_cols, value_cols, row_request, row_position, key_request, key_position
    )
    attention_rows = lax.all_to_all(
        attention.reshape(exp_count, tok_rows, HEAD_DIM), "exp", 0, 0, tiled=True
    )
    attention_rows = attention_rows.transpose(1, 0, 2).reshape(tok_rows, model_width)
    mixed = jnp.dot(attention_rows, whole_proj, preferred_element_type=jnp.float32)
    stream = resid.astype(jnp.float32) + mixed
    normed = rms_normed(stream, norm_gain)

    piece = lax.all_gather(normed, "exp", axis=0, tiled=True)
    hidden_here = shared_gate.shape[1]
    both = jnp.dot(
        piece,
        jnp.concatenate([shared_gate, shared_up], axis=1),
        preferred_element_type=jnp.float32,
    )
    gate = both[:, :hidden_here]
    upper = both[:, hidden_here:]
    shared_hidden = (jax.nn.silu(gate) * upper).astype(jnp.bfloat16)
    shared_part = jnp.dot(
        shared_hidden, shared_down, preferred_element_type=jnp.float32
    ).astype(jnp.bfloat16)
    shared_out = lax.psum_scatter(
        shared_part, "exp", scatter_dimension=0, tiled=True
    ).astype(jnp.float32)
    shared_scale = jax.nn.sigmoid(
        jnp.dot(normed, shared_scalar, preferred_element_type=jnp.float32)
    )

    slot_ids = jnp.arange(slot_count, dtype=jnp.int32)
    same_expert = slot_expert[:, None] == slot_expert[None, :]
    copy_rank = jnp.sum(
        (same_expert & (slot_ids[None, :] < slot_ids[:, None])).astype(jnp.int32), axis=1
    )
    own_routes = lax.dynamic_slice_in_dim(route_expert, own_slot * tok_rows, tok_rows, 0).reshape(
        -1
    )
    holds = own_routes[:, None] == slot_expert[None, :]
    chosen = holds & (copy_rank[None, :] == 0)
    target = jnp.sum(jnp.where(chosen, slot_ids[None, :], 0), axis=1)
    onehot = chosen.astype(jnp.int32)
    position = jnp.sum(jnp.cumsum(onehot, axis=0) * onehot, axis=1) - 1
    buffer_index = target * capacity + position
    entry_rows = jnp.repeat(normed, TOPK, axis=0)
    outgoing = (
        jnp.zeros((slot_count * capacity, model_width), jnp.bfloat16)
        .at[buffer_index]
        .set(entry_rows)
    )
    outgoing = outgoing.reshape(slot_count, capacity, model_width)
    incoming = lax.all_to_all(outgoing, ("req", "exp"), split_axis=0, concat_axis=0, tiled=True)
    answered = expert_block(
        incoming.reshape(-1, model_width), expert_gate[0], expert_up[0], expert_down[0]
    ).reshape(slot_count, capacity, model_width)
    returned = lax.all_to_all(
        answered, ("req", "exp"), split_axis=0, concat_axis=0, tiled=True
    ).reshape(-1, model_width)
    expert_out = returned[buffer_index].reshape(tok_rows, TOPK, model_width)
    routed = jnp.sum(expert_out.astype(jnp.float32) * route_gate[:, :, None], axis=1)
    return (stream + shared_scale[:, None] * shared_out + routed).astype(jnp.bfloat16)


def solution(mesh):
    placed = (
        P(("req", "exp"), None),
        P(("req", "exp"), None),
        P(("req", "exp"), None, None),
        P(("req", "exp"), None, None),
        P("req", None),
        P("req"),
        P("req"),
        P("exp", None),
        P(),
        P(("req", "exp"), None, None),
        P(("req", "exp"), None, None),
        P(("req", "exp"), None, None),
        P(None, "exp"),
        P(None, "exp"),
        P("exp", None),
        P(),
        P(),
        P(),
        P(("req", "exp"), None),
    )
    return jax.shard_map(
        shards, mesh=mesh, in_specs=placed, out_specs=P(("req", "exp"), None), check_vma=False
    )
```

```python
import jax
import jax.numpy as jnp
from jax import lax
from jax.experimental import pallas as pl
from jax.sharding import PartitionSpec as P

HEADS = 16
HEAD_DIM = 128
TOPK = 4


def expert_block(rows, gate_w, up_w, down_w):
    gate = jnp.dot(rows, gate_w, preferred_element_type=jnp.float32)
    upper = jnp.dot(rows, up_w, preferred_element_type=jnp.float32)
    hidden = (jax.nn.silu(gate) * upper).astype(jnp.bfloat16)
    return jnp.dot(hidden, down_w, preferred_element_type=jnp.float32).astype(jnp.bfloat16)


def rms_normed(stream, norm_gain):
    scale_row = lax.rsqrt(jnp.mean(stream * stream, axis=1, keepdims=True) + 1e-06)
    return (stream * scale_row * norm_gain[None, :]).astype(jnp.bfloat16)


def head_attention_kernel(q_ref, k_ref, v_ref, rreq_ref, rpos_ref, kreq_ref, kpos_ref, o_ref):
    scores = lax.dot_general(
        q_ref[...], k_ref[...], (((1,), (1,)), ((), ())), preferred_element_type=jnp.float32
    ) * HEAD_DIM ** (-0.5)
    visible = (rreq_ref[...] == kreq_ref[...]) & (kpos_ref[...] <= rpos_ref[...])
    scores = jnp.where(visible, scores, -1e30)
    top = jnp.max(scores, axis=1, keepdims=True)
    weights = jnp.where(visible, jnp.exp(scores - top), 0.0)
    denominators = jnp.sum(weights, axis=1, keepdims=True)
    numerators = jnp.dot(
        weights.astype(jnp.bfloat16), v_ref[...], preferred_element_type=jnp.float32
    )
    o_ref[...] = (numerators / denominators).astype(o_ref.dtype)


def head_attention(query_cols, key_cols, value_cols, row_request, row_position, key_request, key_position):
    rows, width = query_cols.shape
    keys = key_cols.shape[0]
    tile = 128
    row_spec = pl.BlockSpec((tile, width), lambda i: (i, 0))
    whole = pl.BlockSpec((keys, width), lambda i: (0, 0))
    row_int = pl.BlockSpec((tile, 1), lambda i: (i, 0))
    key_int = pl.BlockSpec((1, keys), lambda i: (0, 0))
    return pl.pallas_call(
        head_attention_kernel,
        grid=(rows // tile,),
        out_shape=jax.ShapeDtypeStruct((rows, width), jnp.bfloat16),
        in_specs=[row_spec, whole, whole, row_int, row_int, key_int, key_int],
        out_specs=row_spec,
        cost_estimate=pl.CostEstimate(
            flops=4 * rows * keys * width, transcendentals=rows * keys, bytes_accessed=3 * keys * width * 2
        ),
    )(
        query_cols,
        key_cols,
        value_cols,
        row_request.reshape(rows, 1),
        row_position.reshape(rows, 1),
        key_request.reshape(1, keys),
        key_position.reshape(1, keys),
    )


def gather_exp(piece, count):
    spread = jnp.broadcast_to(piece[None], (count,) + piece.shape)
    got = lax.all_to_all(spread, "exp", 0, 0, tiled=True)
    return got.reshape((count * piece.shape[0],) + piece.shape[1:])


def shards(
    resid,
    queries,
    cache_key,
    cache_value,
    page_table,
    row_request,
    row_position,
    out_proj,
    norm_gain,
    expert_gate,
    expert_up,
    expert_down,
    shared_gate,
    shared_up,
    shared_down,
    shared_scalar,
    slot_expert,
    route_expert,
    route_gate,
):
    exp_count = lax.axis_size("exp")
    req_count = lax.axis_size("req")
    slot_count = exp_count * req_count
    exp_index = lax.axis_index("exp")
    own_slot = lax.axis_index("req") * exp_count + exp_index
    tok_rows = resid.shape[0]
    model_width = resid.shape[1]
    group_rows = row_request.shape[0]
    pages_here = cache_key.shape[0]
    page_len = cache_key.shape[1]
    req_slots = page_table.shape[0]
    max_pages = page_table.shape[1]
    capacity = 3 * tok_rows * TOPK // slot_count

    whole_proj = lax.all_gather(out_proj, "exp", axis=0, tiled=True)
    key_count = pages_here * page_len
    group_keys = exp_count * key_count
    by_head = jnp.concatenate(
        [
            queries.reshape(tok_rows, HEADS, HEAD_DIM).transpose(1, 0, 2),
            cache_key.reshape(key_count, HEADS, HEAD_DIM).transpose(1, 0, 2),
            cache_value.reshape(key_count, HEADS, HEAD_DIM).transpose(1, 0, 2),
        ],
        axis=1,
    )
    got_cols = lax.all_to_all(by_head, "exp", 0, 0, tiled=True)
    query_cols = got_cols[:, :tok_rows].reshape(group_rows, HEAD_DIM)
    key_cols = got_cols[:, tok_rows:tok_rows + key_count].reshape(group_keys, HEAD_DIM)
    value_cols = got_cols[:, tok_rows + key_count:].reshape(group_keys, HEAD_DIM)
    page_ids = jnp.arange(exp_count * pages_here, dtype=jnp.int32)
    hits = (page_table[None, :, :] == page_ids[:, None, None]).astype(jnp.int32)
    page_request = jnp.sum(
        hits * jnp.arange(req_slots, dtype=jnp.int32)[None, :, None], axis=(1, 2)
    )
    page_slot = jnp.sum(hits * jnp.arange(max_pages, dtype=jnp.int32)[None, None, :], axis=(1, 2))
    key_position = (
        page_slot[:, None] * page_len + jnp.arange(page_len, dtype=jnp.int32)[None, :]
    ).reshape(-1)
    key_request = jnp.repeat(page_request, page_len)
    attention = head_attention(
        query_cols, key_cols, value_cols, row_request, row_position, key_request, key_position
    )
    attention_rows = lax.all_to_all(
        attention.reshape(exp_count, tok_rows, HEAD_DIM), "exp", 0, 0, tiled=True
    )
    attention_rows = attention_rows.transpose(1, 0, 2).reshape(tok_rows, model_width)
    mixed = jnp.dot(attention_rows, whole_proj, preferred_element_type=jnp.float32)
    stream = resid.astype(jnp.float32) + mixed
    normed = rms_normed(stream, norm_gain)

    piece = lax.all_gather(normed, "exp", axis=0, tiled=True)
    hidden_here = shared_gate.shape[1]
    both = jnp.dot(
        piece,
        jnp.concatenate([shared_gate, shared_up], axis=1),
        preferred_element_type=jnp.float32,
    )
    gate = both[:, :hidden_here]
    upper = both[:, hidden_here:]
    shared_hidden = (jax.nn.silu(gate) * upper).astype(jnp.bfloat16)
    shared_part = jnp.dot(
        shared_hidden, shared_down, preferred_element_type=jnp.float32
    ).astype(jnp.bfloat16)
    shared_out = lax.psum_scatter(
        shared_part, "exp", scatter_dimension=0, tiled=True
    ).astype(jnp.float32)
    shared_scale = jax.nn.sigmoid(
        jnp.dot(normed, shared_scalar, preferred_element_type=jnp.float32)
    )

    slot_ids = jnp.arange(slot_count, dtype=jnp.int32)
    same_expert = slot_expert[:, None] == slot_expert[None, :]
    copy_rank = jnp.sum(
        (same_expert & (slot_ids[None, :] < slot_ids[:, None])).astype(jnp.int32), axis=1
    )
    own_routes = lax.dynamic_slice_in_dim(route_expert, own_slot * tok_rows, tok_rows, 0).reshape(
        -1
    )
    holds = own_routes[:, None] == slot_expert[None, :]
    chosen = holds & (copy_rank[None, :] == 0)
    target = jnp.sum(jnp.where(chosen, slot_ids[None, :], 0), axis=1)
    onehot = chosen.astype(jnp.int32)
    position = jnp.sum(jnp.cumsum(onehot, axis=0) * onehot, axis=1) - 1
    places = jnp.arange(capacity, dtype=jnp.int32)
    entry_of = (target[:, None, None] == slot_ids[None, :, None]) & (
        position[:, None, None] == places[None, None, :]
    )
    row_of_entry = jnp.arange(tok_rows * TOPK, dtype=jnp.int32) // TOPK
    row_match = row_of_entry[:, None] == jnp.arange(tok_rows, dtype=jnp.int32)[None, :]
    picks = jnp.einsum(
        "esc,ei->sci",
        entry_of.astype(jnp.bfloat16),
        row_match.astype(jnp.bfloat16),
        preferred_element_type=jnp.float32,
    ).astype(jnp.bfloat16)
    outgoing = jnp.einsum(
        "sci,id->scd", picks, normed, preferred_element_type=jnp.float32
    ).astype(jnp.bfloat16)
    incoming = lax.all_to_all(outgoing, ("req", "exp"), split_axis=0, concat_axis=0, tiled=True)
    answered = expert_block(incoming, expert_gate[0], expert_up[0], expert_down[0])
    returned = lax.all_to_all(answered, ("req", "exp"), split_axis=0, concat_axis=0, tiled=True)
    chosen_rows = jnp.einsum(
        "rksc,scd->rkd",
        entry_of.reshape(tok_rows, TOPK, slot_count, capacity).astype(jnp.bfloat16),
        returned,
        preferred_element_type=jnp.float32,
    )
    routed = jnp.sum(chosen_rows * route_gate[:, :, None], axis=1)
    return (stream + shared_scale[:, None] * shared_out + routed).astype(jnp.bfloat16)


def solution(mesh):
    placed = (
        P(("req", "exp"), None),
        P(("req", "exp"), None),
        P(("req", "exp"), None, None),
        P(("req", "exp"), None, None),
        P("req", None),
        P("req"),
        P("req"),
        P("exp", None),
        P(),
        P(("req", "exp"), None, None),
        P(("req", "exp"), None, None),
        P(("req", "exp"), None, None),
        P(None, "exp"),
        P(None, "exp"),
        P("exp", None),
        P(),
        P(),
        P(),
        P(("req", "exp"), None),
    )
    return jax.shard_map(
        shards, mesh=mesh, in_specs=placed, out_specs=P(("req", "exp"), None), check_vma=False
    )
```

```python
import jax
import jax.numpy as jnp
from jax import lax
from jax.experimental import pallas as pl
from jax.sharding import PartitionSpec as P

HEADS = 16
HEAD_DIM = 128
TOPK = 4


def expert_block(rows, gate_w, up_w, down_w):
    gate = jnp.dot(rows, gate_w, preferred_element_type=jnp.float32)
    upper = jnp.dot(rows, up_w, preferred_element_type=jnp.float32)
    hidden = (jax.nn.silu(gate) * upper).astype(jnp.bfloat16)
    return jnp.dot(hidden, down_w, preferred_element_type=jnp.float32).astype(jnp.bfloat16)


def rms_normed(stream, norm_gain):
    scale_row = lax.rsqrt(jnp.mean(stream * stream, axis=1, keepdims=True) + 1e-06)
    return (stream * scale_row * norm_gain[None, :]).astype(jnp.bfloat16)


def head_attention_kernel(q_ref, k_ref, v_ref, rreq_ref, rpos_ref, kreq_ref, kpos_ref, o_ref):
    scores = lax.dot_general(
        q_ref[...], k_ref[...], (((1,), (1,)), ((), ())), preferred_element_type=jnp.float32
    ) * HEAD_DIM ** (-0.5)
    visible = (rreq_ref[...] == kreq_ref[...]) & (kpos_ref[...] <= rpos_ref[...])
    scores = jnp.where(visible, scores, -1e30)
    top = jnp.max(scores, axis=1, keepdims=True)
    weights = jnp.where(visible, jnp.exp(scores - top), 0.0)
    denominators = jnp.sum(weights, axis=1, keepdims=True)
    numerators = jnp.dot(
        weights.astype(jnp.bfloat16), v_ref[...], preferred_element_type=jnp.float32
    )
    o_ref[...] = (numerators / denominators).astype(o_ref.dtype)


def head_attention(query_cols, key_cols, value_cols, row_request, row_position, key_request, key_position):
    rows, width = query_cols.shape
    keys = key_cols.shape[0]
    tile = 128
    row_spec = pl.BlockSpec((tile, width), lambda i: (i, 0))
    whole = pl.BlockSpec((keys, width), lambda i: (0, 0))
    row_int = pl.BlockSpec((tile, 1), lambda i: (i, 0))
    key_int = pl.BlockSpec((1, keys), lambda i: (0, 0))
    return pl.pallas_call(
        head_attention_kernel,
        grid=(rows // tile,),
        out_shape=jax.ShapeDtypeStruct((rows, width), jnp.bfloat16),
        in_specs=[row_spec, whole, whole, row_int, row_int, key_int, key_int],
        out_specs=row_spec,
        cost_estimate=pl.CostEstimate(
            flops=4 * rows * keys * width, transcendentals=rows * keys, bytes_accessed=3 * keys * width * 2
        ),
    )(
        query_cols,
        key_cols,
        value_cols,
        row_request.reshape(rows, 1),
        row_position.reshape(rows, 1),
        key_request.reshape(1, keys),
        key_position.reshape(1, keys),
    )


def gather_exp(piece, count):
    spread = jnp.broadcast_to(piece[None], (count,) + piece.shape)
    got = lax.all_to_all(spread, "exp", 0, 0, tiled=True)
    return got.reshape((count * piece.shape[0],) + piece.shape[1:])


def shards(
    resid,
    queries,
    cache_key,
    cache_value,
    page_table,
    row_request,
    row_position,
    out_proj,
    norm_gain,
    expert_gate,
    expert_up,
    expert_down,
    shared_gate,
    shared_up,
    shared_down,
    shared_scalar,
    slot_expert,
    route_expert,
    route_gate,
):
    exp_count = lax.axis_size("exp")
    req_count = lax.axis_size("req")
    slot_count = exp_count * req_count
    exp_index = lax.axis_index("exp")
    own_slot = lax.axis_index("req") * exp_count + exp_index
    tok_rows = resid.shape[0]
    model_width = resid.shape[1]
    group_rows = row_request.shape[0]
    pages_here = cache_key.shape[0]
    page_len = cache_key.shape[1]
    req_slots = page_table.shape[0]
    max_pages = page_table.shape[1]
    capacity = 3 * tok_rows * TOPK // slot_count

    whole_proj = lax.all_gather(out_proj, "exp", axis=0, tiled=True)
    key_count = pages_here * page_len
    group_keys = exp_count * key_count
    by_head = jnp.concatenate(
        [
            queries.reshape(tok_rows, HEADS, HEAD_DIM).transpose(1, 0, 2),
            cache_key.reshape(key_count, HEADS, HEAD_DIM).transpose(1, 0, 2),
            cache_value.reshape(key_count, HEADS, HEAD_DIM).transpose(1, 0, 2),
        ],
        axis=1,
    )
    got_cols = lax.all_to_all(by_head, "exp", 0, 0, tiled=True)
    query_cols = got_cols[:, :tok_rows].reshape(group_rows, HEAD_DIM)
    key_cols = got_cols[:, tok_rows:tok_rows + key_count].reshape(group_keys, HEAD_DIM)
    value_cols = got_cols[:, tok_rows + key_count:].reshape(group_keys, HEAD_DIM)
    page_ids = jnp.arange(exp_count * pages_here, dtype=jnp.int32)
    hits = (page_table[None, :, :] == page_ids[:, None, None]).astype(jnp.int32)
    page_request = jnp.sum(
        hits * jnp.arange(req_slots, dtype=jnp.int32)[None, :, None], axis=(1, 2)
    )
    page_slot = jnp.sum(hits * jnp.arange(max_pages, dtype=jnp.int32)[None, None, :], axis=(1, 2))
    key_position = (
        page_slot[:, None] * page_len + jnp.arange(page_len, dtype=jnp.int32)[None, :]
    ).reshape(-1)
    key_request = jnp.repeat(page_request, page_len)
    attention = head_attention(
        query_cols, key_cols, value_cols, row_request, row_position, key_request, key_position
    )
    attention_rows = lax.all_to_all(
        attention.reshape(exp_count, tok_rows, HEAD_DIM), "exp", 0, 0, tiled=True
    )
    attention_rows = attention_rows.transpose(1, 0, 2).reshape(tok_rows, model_width)
    mixed = jnp.dot(attention_rows, whole_proj, preferred_element_type=jnp.float32)
    stream = resid.astype(jnp.float32) + mixed
    normed = rms_normed(stream, norm_gain)

    piece = lax.all_gather(normed, "exp", axis=0, tiled=True)
    hidden_here = shared_gate.shape[1]
    both = jnp.dot(
        piece,
        jnp.concatenate([shared_gate, shared_up], axis=1),
        preferred_element_type=jnp.float32,
    )
    gate = both[:, :hidden_here]
    upper = both[:, hidden_here:]
    shared_hidden = (jax.nn.silu(gate) * upper).astype(jnp.bfloat16)
    shared_part = jnp.dot(
        shared_hidden, shared_down, preferred_element_type=jnp.float32
    ).astype(jnp.bfloat16)
    shared_out = lax.psum_scatter(
        shared_part, "exp", scatter_dimension=0, tiled=True
    ).astype(jnp.float32)
    shared_scale = jax.nn.sigmoid(
        jnp.dot(normed, shared_scalar, preferred_element_type=jnp.float32)
    )

    slot_ids = jnp.arange(slot_count, dtype=jnp.int32)
    same_expert = slot_expert[:, None] == slot_expert[None, :]
    copy_rank = jnp.sum(
        (same_expert & (slot_ids[None, :] < slot_ids[:, None])).astype(jnp.int32), axis=1
    )
    own_routes = lax.dynamic_slice_in_dim(route_expert, own_slot * tok_rows, tok_rows, 0).reshape(
        -1
    )
    holds = own_routes[:, None] == slot_expert[None, :]
    chosen = holds & (copy_rank[None, :] == 0)
    target = jnp.sum(jnp.where(chosen, slot_ids[None, :], 0), axis=1)
    onehot = chosen.astype(jnp.int32)
    position = jnp.sum(jnp.cumsum(onehot, axis=0) * onehot, axis=1) - 1
    buffer_index = target * capacity + position
    entry_rows = jnp.repeat(normed, TOPK, axis=0)
    outgoing = (
        jnp.zeros((slot_count * capacity, model_width), jnp.bfloat16)
        .at[buffer_index]
        .set(entry_rows)
    )
    outgoing = outgoing.reshape(slot_count, capacity, model_width)
    incoming = lax.all_to_all(outgoing, ("req", "exp"), split_axis=0, concat_axis=0, tiled=True)
    answered = expert_block(
        incoming.reshape(-1, model_width), expert_gate[0], expert_up[0], expert_down[0]
    ).reshape(slot_count, capacity, model_width)
    returned = lax.all_to_all(
        answered, ("req", "exp"), split_axis=0, concat_axis=0, tiled=True
    )
    entry_of = (target[:, None, None] == slot_ids[None, :, None]) & (
        position[:, None, None] == jnp.arange(capacity, dtype=jnp.int32)[None, None, :]
    )
    chosen_rows = jnp.einsum(
        "rksc,scd->rkd",
        entry_of.reshape(tok_rows, TOPK, slot_count, capacity).astype(jnp.bfloat16),
        returned,
        preferred_element_type=jnp.float32,
    )
    routed = jnp.sum(chosen_rows * route_gate[:, :, None], axis=1)
    return (stream + shared_scale[:, None] * shared_out + routed).astype(jnp.bfloat16)


def solution(mesh):
    placed = (
        P(("req", "exp"), None),
        P(("req", "exp"), None),
        P(("req", "exp"), None, None),
        P(("req", "exp"), None, None),
        P("req", None),
        P("req"),
        P("req"),
        P("exp", None),
        P(),
        P(("req", "exp"), None, None),
        P(("req", "exp"), None, None),
        P(("req", "exp"), None, None),
        P(None, "exp"),
        P(None, "exp"),
        P("exp", None),
        P(),
        P(),
        P(),
        P(("req", "exp"), None),
    )
    return jax.shard_map(
        shards, mesh=mesh, in_specs=placed, out_specs=P(("req", "exp"), None), check_vma=False
    )
```

```python
import jax
import jax.numpy as jnp
from jax import lax
from jax.experimental import pallas as pl
from jax.sharding import PartitionSpec as P

HEADS = 16
HEAD_DIM = 128
TOPK = 4


def expert_block(rows, gate_w, up_w, down_w):
    gate = jnp.dot(rows, gate_w, preferred_element_type=jnp.float32)
    upper = jnp.dot(rows, up_w, preferred_element_type=jnp.float32)
    hidden = (jax.nn.silu(gate) * upper).astype(jnp.bfloat16)
    return jnp.dot(hidden, down_w, preferred_element_type=jnp.float32).astype(jnp.bfloat16)


def rms_normed(stream, norm_gain):
    scale_row = lax.rsqrt(jnp.mean(stream * stream, axis=1, keepdims=True) + 1e-06)
    return (stream * scale_row * norm_gain[None, :]).astype(jnp.bfloat16)


def head_attention_kernel(q_ref, k_ref, v_ref, rreq_ref, rpos_ref, kreq_ref, kpos_ref, o_ref):
    scores = lax.dot_general(
        q_ref[...], k_ref[...], (((1,), (1,)), ((), ())), preferred_element_type=jnp.float32
    ) * HEAD_DIM ** (-0.5)
    visible = (rreq_ref[...] == kreq_ref[...]) & (kpos_ref[...] <= rpos_ref[...])
    scores = jnp.where(visible, scores, -1e30)
    top = jnp.max(scores, axis=1, keepdims=True)
    weights = jnp.where(visible, jnp.exp(scores - top), 0.0)
    denominators = jnp.sum(weights, axis=1, keepdims=True)
    numerators = jnp.dot(
        weights.astype(jnp.bfloat16), v_ref[...], preferred_element_type=jnp.float32
    )
    o_ref[...] = (numerators / denominators).astype(o_ref.dtype)


def head_attention(query_cols, key_cols, value_cols, row_request, row_position, key_request, key_position):
    rows, width = query_cols.shape
    keys = key_cols.shape[0]
    tile = 256
    row_spec = pl.BlockSpec((tile, width), lambda i: (i, 0))
    whole = pl.BlockSpec((keys, width), lambda i: (0, 0))
    row_int = pl.BlockSpec((tile, 1), lambda i: (i, 0))
    key_int = pl.BlockSpec((1, keys), lambda i: (0, 0))
    return pl.pallas_call(
        head_attention_kernel,
        grid=(rows // tile,),
        out_shape=jax.ShapeDtypeStruct((rows, width), jnp.bfloat16),
        in_specs=[row_spec, whole, whole, row_int, row_int, key_int, key_int],
        out_specs=row_spec,
        cost_estimate=pl.CostEstimate(
            flops=4 * rows * keys * width, transcendentals=rows * keys, bytes_accessed=3 * keys * width * 2
        ),
    )(
        query_cols,
        key_cols,
        value_cols,
        row_request.reshape(rows, 1),
        row_position.reshape(rows, 1),
        key_request.reshape(1, keys),
        key_position.reshape(1, keys),
    )


def gather_exp(piece, count):
    spread = jnp.broadcast_to(piece[None], (count,) + piece.shape)
    got = lax.all_to_all(spread, "exp", 0, 0, tiled=True)
    return got.reshape((count * piece.shape[0],) + piece.shape[1:])


def shards(
    resid,
    queries,
    cache_key,
    cache_value,
    page_table,
    row_request,
    row_position,
    out_proj,
    norm_gain,
    expert_gate,
    expert_up,
    expert_down,
    shared_gate,
    shared_up,
    shared_down,
    shared_scalar,
    slot_expert,
    route_expert,
    route_gate,
):
    exp_count = lax.axis_size("exp")
    req_count = lax.axis_size("req")
    slot_count = exp_count * req_count
    exp_index = lax.axis_index("exp")
    own_slot = lax.axis_index("req") * exp_count + exp_index
    tok_rows = resid.shape[0]
    model_width = resid.shape[1]
    group_rows = row_request.shape[0]
    pages_here = cache_key.shape[0]
    page_len = cache_key.shape[1]
    req_slots = page_table.shape[0]
    max_pages = page_table.shape[1]
    capacity = 3 * tok_rows * TOPK // slot_count

    whole_proj = lax.all_gather(out_proj, "exp", axis=0, tiled=True)
    key_count = pages_here * page_len
    group_keys = exp_count * key_count
    by_head = jnp.concatenate(
        [
            queries.reshape(tok_rows, HEADS, HEAD_DIM).transpose(1, 0, 2),
            cache_key.reshape(key_count, HEADS, HEAD_DIM).transpose(1, 0, 2),
            cache_value.reshape(key_count, HEADS, HEAD_DIM).transpose(1, 0, 2),
        ],
        axis=1,
    )
    got_cols = lax.all_to_all(by_head, "exp", 0, 0, tiled=True)
    query_cols = got_cols[:, :tok_rows].reshape(group_rows, HEAD_DIM)
    key_cols = got_cols[:, tok_rows:tok_rows + key_count].reshape(group_keys, HEAD_DIM)
    value_cols = got_cols[:, tok_rows + key_count:].reshape(group_keys, HEAD_DIM)
    page_ids = jnp.arange(exp_count * pages_here, dtype=jnp.int32)
    hits = (page_table[None, :, :] == page_ids[:, None, None]).astype(jnp.int32)
    page_request = jnp.sum(
        hits * jnp.arange(req_slots, dtype=jnp.int32)[None, :, None], axis=(1, 2)
    )
    page_slot = jnp.sum(hits * jnp.arange(max_pages, dtype=jnp.int32)[None, None, :], axis=(1, 2))
    key_position = (
        page_slot[:, None] * page_len + jnp.arange(page_len, dtype=jnp.int32)[None, :]
    ).reshape(-1)
    key_request = jnp.repeat(page_request, page_len)
    attention = head_attention(
        query_cols, key_cols, value_cols, row_request, row_position, key_request, key_position
    )
    attention_rows = lax.all_to_all(
        attention.reshape(exp_count, tok_rows, HEAD_DIM), "exp", 0, 0, tiled=True
    )
    attention_rows = attention_rows.transpose(1, 0, 2).reshape(tok_rows, model_width)
    mixed = jnp.dot(attention_rows, whole_proj, preferred_element_type=jnp.float32)
    stream = resid.astype(jnp.float32) + mixed
    normed = rms_normed(stream, norm_gain)

    piece = lax.all_gather(normed, "exp", axis=0, tiled=True)
    hidden_here = shared_gate.shape[1]
    both = jnp.dot(
        piece,
        jnp.concatenate([shared_gate, shared_up], axis=1),
        preferred_element_type=jnp.float32,
    )
    gate = both[:, :hidden_here]
    upper = both[:, hidden_here:]
    shared_hidden = (jax.nn.silu(gate) * upper).astype(jnp.bfloat16)
    shared_part = jnp.dot(
        shared_hidden, shared_down, preferred_element_type=jnp.float32
    ).astype(jnp.bfloat16)
    shared_out = lax.psum_scatter(
        shared_part, "exp", scatter_dimension=0, tiled=True
    ).astype(jnp.float32)
    shared_scale = jax.nn.sigmoid(
        jnp.dot(normed, shared_scalar, preferred_element_type=jnp.float32)
    )

    slot_ids = jnp.arange(slot_count, dtype=jnp.int32)
    same_expert = slot_expert[:, None] == slot_expert[None, :]
    copy_rank = jnp.sum(
        (same_expert & (slot_ids[None, :] < slot_ids[:, None])).astype(jnp.int32), axis=1
    )
    own_routes = lax.dynamic_slice_in_dim(route_expert, own_slot * tok_rows, tok_rows, 0).reshape(
        -1
    )
    holds = own_routes[:, None] == slot_expert[None, :]
    chosen = holds & (copy_rank[None, :] == 0)
    target = jnp.sum(jnp.where(chosen, slot_ids[None, :], 0), axis=1)
    onehot = chosen.astype(jnp.int32)
    position = jnp.sum(jnp.cumsum(onehot, axis=0) * onehot, axis=1) - 1
    buffer_index = target * capacity + position
    entry_rows = jnp.repeat(normed, TOPK, axis=0)
    outgoing = (
        jnp.zeros((slot_count * capacity, model_width), jnp.bfloat16)
        .at[buffer_index]
        .set(entry_rows)
    )
    outgoing = outgoing.reshape(slot_count, capacity, model_width)
    incoming = lax.all_to_all(outgoing, ("req", "exp"), split_axis=0, concat_axis=0, tiled=True)
    answered = expert_block(
        incoming.reshape(-1, model_width), expert_gate[0], expert_up[0], expert_down[0]
    ).reshape(slot_count, capacity, model_width)
    returned = lax.all_to_all(
        answered, ("req", "exp"), split_axis=0, concat_axis=0, tiled=True
    ).reshape(-1, model_width)
    expert_out = returned[buffer_index].reshape(tok_rows, TOPK, model_width)
    routed = jnp.sum(expert_out.astype(jnp.float32) * route_gate[:, :, None], axis=1)
    return (stream + shared_scale[:, None] * shared_out + routed).astype(jnp.bfloat16)


def solution(mesh):
    placed = (
        P(("req", "exp"), None),
        P(("req", "exp"), None),
        P(("req", "exp"), None, None),
        P(("req", "exp"), None, None),
        P("req", None),
        P("req"),
        P("req"),
        P("exp", None),
        P(),
        P(("req", "exp"), None, None),
        P(("req", "exp"), None, None),
        P(("req", "exp"), None, None),
        P(None, "exp"),
        P(None, "exp"),
        P("exp", None),
        P(),
        P(),
        P(),
        P(("req", "exp"), None),
    )
    return jax.shard_map(
        shards, mesh=mesh, in_specs=placed, out_specs=P(("req", "exp"), None), check_vma=False
    )
```
